32 devices in a mesh: groups: 2 (over y), ctx: 4 (over z), exp: 4 (over x, core), rep: 1.
Axes of the slice: x: 2, y: 2, z: 4, core: 2. Of those that a mesh axis runs over, the one named last changes fastest.
Arguments:
- queries: bfloat16 [2, 256, 4096], P('groups', 'ctx', ('exp', 'rep')), parts along dimension 0, may hold values from -16.25 to 16.25
- pages: bfloat16 [2, 2304, 2, 512], P('groups', 'ctx', None, 'exp'), parts along dimension 0, may hold values from -5.2 to 5.2
- cached_lengths: int32 [2, 4], P('groups'), parts along dimension 0, may hold values from 128 to 512
- residual_in: bfloat16 [2, 256, 2048], P('groups', ('ctx', 'exp')), parts along dimension 0, may hold values from -2.390625 to 2.390625
- out_weight: bfloat16 [4096, 2048], P(('exp', 'rep')), may hold values from -0.09375 to 0.09375
- norm_gain: float32 [2048], replicated, may hold values from 0.1 to 1.9
- expert_ids: int32 [2, 256, 8], P('groups', ('ctx', 'exp')), parts along dimension 0, may hold values from 0 to 15, all different within a row; in each aligned block of 16 rows (0 to 15, 16 to 31, ..., all dimensions but the last counted through in order) at most 8 rows name the same one
- route_scores: float32 [2, 256, 8], P('groups', ('ctx', 'exp')), parts along dimension 0, may hold values from 0.05 to 1
- expert_input: bfloat16 [16, 2048, 2, 384], P(('ctx', 'exp'), None, None, 'rep'), may hold values from -0.125 to 0.125
- expert_output: bfloat16 [16, 384, 2048], P(('ctx', 'exp'), 'rep'), may hold values from -0.3125 to 0.3125
Outputs:
- context: bfloat16 [2, 256, 4096], P('groups', 'ctx', ('exp', 'rep')), parts along dimension 0
- layer_out: bfloat16 [2, 256, 2048], P('groups', ('ctx', 'exp', 'rep')), parts along dimension 0
The draws below stay inside these ranges and needn't reach their ends.
There are 2 independent parts, one for each index of `groups`. The reference program is written for one: setup_inputs(seed, part) draws one part's arguments, and reference() takes and returns one part's arrays. A program takes and returns all parts, laid end to end along the dimension named above; an argument that names none is the same for every part. Nothing has to cross between parts.
Inputs may be any that keep to these rules, and one draw needn't show every extreme that they name: `expert_ids`: in every aligned block of 16 positions of one request, no expert is named by more than 8 of the block's rows, and in some blocks one expert by exactly 8; the 8 experts of a row differ.
All inputs are finite; a program needn't handle non-finite values.
Results may differ from the reference program's by a relative error of at most 0.015.
Values may be sent and summed in bfloat16 or wider, within the bound.
A program may use at most 128 MiB of HBM per device.

```python
import math
import jax
import jax.numpy as jnp
import numpy as np
from jax import lax

D = 2048
HEADS = 32
KV_HEADS = 4
HEAD = 128
TOPK = 8
EXPERT_FF = 384
REQS = 1
FRESH_DEV = 64
SLAB = 512
FRESH = 256
PAGE = 576
PAGE_COUNT = 4
PAGES_LEN = 2304
EXPERTS = 16
TOK_BLK = 16
MOST = 8
SPLITS = 1


def draw_queries(key, part):
    values = 2.0 * jax.random.normal(jax.random.fold_in(key, 11), (REQS, FRESH, HEADS * HEAD), jnp.float32)
    values = jnp.clip(values, -8.0, 8.0)
    return values.astype(jnp.bfloat16)


def draw_pages(key, part):
    values = 1.3 * jax.random.normal(jax.random.fold_in(key, 12), (REQS, PAGES_LEN, 2, KV_HEADS * HEAD), jnp.float32)
    values = jnp.clip(values, -5.2, 5.2)
    return values.astype(jnp.bfloat16)


def draw_cached_lengths(key, part):
    slab_count = PAGES_LEN // PAGE
    lowest = max(2, SLAB // 4)
    drawn_lengths = jax.random.randint(jax.random.fold_in(key, 13), (REQS, slab_count), lowest, SLAB + 1)
    full_pick = jax.random.randint(jax.random.fold_in(key, 14), (REQS, 1), 0, slab_count)
    filled = jnp.where(jnp.arange(slab_count, dtype=jnp.int32)[None, :] == full_pick, SLAB, drawn_lengths)
    return filled.astype(jnp.int32)


def level_of(stream_key, shape, pieces, least, top_value):
    loudness, own = 1.0, jax.random.fold_in(stream_key, 6)
    for position, parts in pieces:
        steps = jnp.exp(jax.random.uniform(jax.random.fold_in(own, position), (parts,), jnp.float32, least / len(pieces), top_value / len(pieces)))
        loudness = loudness * jnp.repeat(steps, shape[position] // parts).reshape([-1 if axis == position else 1 for axis in range(len(shape))])
    return loudness


def routed_block(rng, own, number, rows, count, top, bound, lean):
    ranking = jax.random.permutation(rng, count)
    heavy_load, ordinary = shares(count, rows * top, bound, lean, True), shares(count, rows * top, bound, lean, False)
    places = jnp.arange(count)

    def named(tallies, turn):
        used = int((tallies > 0).sum())
        fixed = max(1, used // 4)
        shifted = fixed + (places - fixed + turn * (used - fixed)) % max(1, count - fixed)
        return jnp.zeros((count,), jnp.int32).at[ranking[jnp.where(places < fixed, places, shifted)]].set(jnp.asarray(tallies, jnp.int32))

    tallies = jnp.where(number % 4 == 0, named(heavy_load, number // 4), named(ordinary, number - number // 4 - 1))
    mixed = jax.random.permutation(jax.random.fold_in(own, 3), count)
    donor, taker = mixed[0:count // 2 * 2:2], mixed[1:count // 2 * 2:2]
    room = jnp.minimum(tallies[donor] - 1, bound - tallies[taker]) // 2
    room = jnp.where((donor == ranking[0]) | (taker == ranking[0]) | (tallies[taker] == 0), 0, jnp.maximum(room, 0))
    shifted = jax.random.randint(jax.random.fold_in(own, 4), (count // 2,), 0, 1 << 20) % (room + 1)
    tallies = tallies.at[donor].add(-shifted).at[taker].add(shifted)
    labels = jnp.searchsorted(jnp.cumsum(tallies), jnp.arange(rows * top), side="right").astype(jnp.int32)
    listing = labels.reshape(top, rows).T
    listing = listing[jax.random.permutation(jax.random.fold_in(own, 1), rows)]
    turn = jax.random.randint(jax.random.fold_in(own, 2), (rows, 1), 0, top)
    return jnp.take_along_axis(listing, (jnp.arange(top)[None, :] + turn) % top, axis=1)


def shares(number_of, total, reach, skew, full):
    weights = [(1 << 20) // math.isqrt(standing ** skew) + 1 for standing in range(1, number_of + 1)]
    largest = reach if full else min(reach, max(-(-total // number_of), total * weights[0] // sum(weights)))
    least = 1 if total - largest >= number_of - 1 else 0
    given, surplus = [largest] + [least] * (number_of - 1), total - largest - least * (number_of - 1)
    while surplus > 0:
        free = [i for i in range(1, number_of) if given[i] < largest] or [i for i in range(1, number_of) if given[i] < reach]
        pool, left = sum([weights[i] for i in free]), surplus
        for i in free:
            more = min(reach - given[i], max(1, left * weights[i] // pool), surplus)
            given[i] = given[i] + more
            surplus = surplus - more
    return np.array(given)


def bell_draw(rng, dims, scale, limit, pieces=(), kind=jnp.bfloat16):
    drawn = jax.random.normal(rng, dims, jnp.float32) * scale
    if len(pieces) > 0:
        drawn = level_of(rng, dims, pieces, -0.22, 0.18) * drawn
    return jnp.clip(drawn, min=-limit, max=limit).astype(kind)


def setup_inputs(seed: int = 0, part: int = 0) -> dict:
    key_list = jax.random.split(jax.random.key(seed), 11)
    own_keys = jax.random.split(jax.random.fold_in(key_list[10], part), 11)
    queries = draw_queries(jax.random.fold_in(jax.random.fold_in(key_list[10], part), 71), part)
    pages = draw_pages(jax.random.fold_in(jax.random.fold_in(key_list[10], part), 71), part)
    cached_lengths = draw_cached_lengths(jax.random.fold_in(jax.random.fold_in(key_list[10], part), 71), part)
    residual_in = bell_draw(own_keys[3], (REQS, FRESH, D), 0.4, 2.390625, ((1, 16),))
    out_weight = bell_draw(key_list[4], (HEADS * HEAD, D), (HEADS * HEAD) ** -0.5, 0.09375, ((0, 4),))
    norm_gain = jnp.clip(1.0 + 0.18 * jax.random.normal(key_list[5], (D,), jnp.float32), 0.1, 1.9)
    expert_ids_keys = jax.random.split(jax.random.fold_in(own_keys[6], 1), REQS * FRESH // TOK_BLK)
    expert_ids_turns = jax.random.permutation(jax.random.fold_in(own_keys[6], 3), REQS * FRESH // TOK_BLK)
    expert_ids = jax.vmap(lambda own, number: routed_block(jax.random.fold_in(own_keys[6], 2), own, number, TOK_BLK, EXPERTS, TOPK, MOST, 2))(expert_ids_keys, expert_ids_turns).reshape((REQS, FRESH, TOPK))
    route_scores = jnp.clip(jnp.exp(math.log(1.0) - 2.9957323 * jax.random.uniform(own_keys[7], (REQS, FRESH, TOPK), jnp.float32) ** level_of(own_keys[7], (REQS, FRESH, TOPK), ((1, 16),), -0.2, 0.2)), 0.05, 1.0)
    expert_input = bell_draw(key_list[8], (EXPERTS, D, 2, EXPERT_FF), D ** -0.5, 0.125, ((0, 16),))
    expert_output = bell_draw(key_list[9], (EXPERTS, EXPERT_FF, D), EXPERT_FF ** -0.5, 0.3125, ((0, 16),))
    return dict(queries=queries, pages=pages, cached_lengths=cached_lengths, residual_in=residual_in, out_weight=out_weight, norm_gain=norm_gain, expert_ids=expert_ids, route_scores=route_scores, expert_input=expert_input, expert_output=expert_output)


floor_value = -1e+30
norm_epsilon = 1e-06

def normalize(hidden, norm_gain):
    widened = hidden.astype(jnp.float32)
    mean_square = lax.optimization_barrier(jnp.mean(widened * widened, axis=-1, keepdims=True))
    return (widened * lax.rsqrt(mean_square + norm_epsilon) * norm_gain).astype(jnp.bfloat16)

def expert_apply(normed_rows, weight_in, weight_out):
    inner_rows = jnp.einsum('nd,dgh->ngh', normed_rows.astype(jnp.float32), weight_in.astype(jnp.float32))
    activated = (jax.nn.silu(inner_rows[:, 0]) * inner_rows[:, 1]).astype(jnp.bfloat16)
    part_width = EXPERT_FF // SPLITS
    result = jnp.zeros((normed_rows.shape[0], D), jnp.float32)
    for portion in range(SPLITS):
        lower = portion * part_width
        partial_value = jnp.dot(activated[:, lower:lower + part_width], weight_out[lower:lower + part_width], preferred_element_type=jnp.float32)
        rounded_part = lax.optimization_barrier(partial_value.astype(jnp.bfloat16))
        result = result + rounded_part.astype(jnp.float32)
    return result

def reference(queries, pages, cached_lengths, residual_in, out_weight, norm_gain, expert_ids, route_scores, expert_input, expert_output):
    group_size = HEADS // KV_HEADS
    scaling = HEAD ** (-0.5)
    zero_index = jnp.int32(0)
    row_index = jnp.arange(PAGES_LEN, dtype=jnp.int32)
    page_number = row_index // PAGE
    offset = row_index - page_number * PAGE
    query_positions = jnp.arange(FRESH, dtype=jnp.int32)

    def one_head(flat_index):
        flat_index = flat_index.astype(jnp.int32)
        request = (flat_index // HEADS).astype(jnp.int32)
        head_number = (flat_index - request * HEADS).astype(jnp.int32)
        pair_head = (head_number // group_size).astype(jnp.int32)
        query_rows = lax.dynamic_slice(queries, (request, zero_index, (head_number * HEAD).astype(jnp.int32)), (1, FRESH, HEAD))[0]
        page_rows = lax.dynamic_slice(pages, (request, zero_index, zero_index, (pair_head * HEAD).astype(jnp.int32)), (1, PAGES_LEN, 2, HEAD))[0]
        lengths_row = lax.dynamic_slice(cached_lengths, (request, zero_index), (1, PAGE_COUNT))[0]
        live_length = lengths_row[page_number]
        in_cache = (offset < SLAB) & (offset < live_length)
        fresh_position = page_number * FRESH_DEV + offset - SLAB
        in_fresh = (offset >= SLAB)[None, :] & (fresh_position[None, :] <= query_positions[:, None])
        allowed = in_cache[None, :] | in_fresh
        scores = jnp.dot(query_rows, page_rows[:, 0].T, preferred_element_type=jnp.float32) * scaling
        masked = jnp.where(allowed, scores, floor_value)
        peaks = lax.optimization_barrier(jnp.max(masked, axis=1, keepdims=True))
        weights = jnp.where(allowed, jnp.exp(masked - peaks), 0.0)
        totals = lax.optimization_barrier(jnp.sum(weights, axis=1, keepdims=True))
        summed = jnp.dot(weights.astype(jnp.bfloat16), page_rows[:, 1], preferred_element_type=jnp.float32)
        return (summed / totals).astype(jnp.bfloat16)
    heads_out = lax.map(one_head, jnp.arange(REQS * HEADS, dtype=jnp.int32))
    context = heads_out.reshape(REQS, HEADS, FRESH, HEAD).transpose(0, 2, 1, 3).reshape(REQS, FRESH, HEADS * HEAD)
    projected = jnp.dot(context.reshape(REQS * FRESH, HEADS * HEAD), out_weight, preferred_element_type=jnp.float32).reshape(REQS, FRESH, D)
    hidden = (residual_in.astype(jnp.float32) + projected).astype(jnp.bfloat16)
    normed = normalize(hidden, norm_gain)
    token_count = REQS * FRESH
    flat_normed = normed.reshape(token_count, D)
    flat_ids = expert_ids.reshape(-1).astype(jnp.int32)
    combine = (route_scores / lax.optimization_barrier(jnp.sum(route_scores, axis=2, keepdims=True))).astype(jnp.bfloat16)
    combine = lax.optimization_barrier(combine).astype(jnp.float32).reshape(-1)
    sorted_rows = jnp.argsort(flat_ids, stable=True).astype(jnp.int32)
    counts = lax.optimization_barrier(jnp.sum((flat_ids[:, None] == jnp.arange(EXPERTS, dtype=jnp.int32)[None, :]).astype(jnp.int32), axis=0))
    starts = (jnp.cumsum(counts) - counts).astype(jnp.int32)
    row_limit = min(token_count * TOPK, token_count // TOK_BLK * MOST)
    padded = jnp.concatenate([sorted_rows, jnp.zeros((row_limit,), jnp.int32)])

    def add_expert(expert, mixture):
        picked = lax.dynamic_slice(padded, (starts[expert].astype(jnp.int32),), (row_limit,))
        alive_rows = jnp.arange(row_limit, dtype=jnp.int32) < counts[expert]
        tokens = picked // TOPK
        outputs = expert_apply(flat_normed[tokens], expert_input[expert], expert_output[expert])
        scaled = outputs * jnp.where(alive_rows, combine[picked], 0.0)[:, None]
        return mixture.at[tokens].add(scaled)
    mixture = lax.fori_loop(0, EXPERTS, add_expert, jnp.zeros((token_count, D), jnp.float32))
    layer_out = (hidden.astype(jnp.float32).reshape(token_count, D) + mixture).astype(jnp.bfloat16).reshape(REQS, FRESH, D)
    return (context, layer_out)
```

```python
import functools

import jax
import jax.numpy as jnp
from jax import lax
from jax.experimental import pallas as pl
from jax.experimental.pallas import tpu as pltpu
from jax.sharding import PartitionSpec as P

HEAD = 128


floor_value = -1e30
norm_epsilon = 1e-06


def normalize(hidden, norm_gain):
    widened = hidden.astype(jnp.float32)
    mean_square = jnp.mean(widened * widened, axis=-1, keepdims=True)
    return (widened * lax.rsqrt(mean_square + norm_epsilon) * norm_gain).astype(jnp.bfloat16)


def attend_piece(query_rows, page_rows, allowed):
    scaling = query_rows.shape[-1] ** (-0.5)
    scores = (
        jnp.einsum(
            "rqhe,rke->rqhk", query_rows, page_rows[:, :, 0], preferred_element_type=jnp.float32
        )
        * scaling
    )
    permitted = allowed[:, :, None, :]
    masked = jnp.where(permitted, scores, floor_value)
    peaks = jnp.max(masked, axis=-1)
    weights = jnp.where(permitted, jnp.exp(masked - peaks[..., None]), 0.0)
    totals = jnp.sum(weights, axis=-1)
    summed = jnp.einsum(
        "rqhk,rke->rqhe",
        weights.astype(jnp.bfloat16),
        page_rows[:, :, 1],
        preferred_element_type=jnp.float32,
    )
    return (peaks, totals, summed)


def merge_partials(earlier, later):
    peaks = jnp.maximum(earlier[0], later[0])
    later_scale = jnp.exp(later[0] - peaks)
    totals = later[1] * later_scale
    summed = later[2] * later_scale[..., None]
    return (peaks, totals, summed)


def rows_mask(row_index, lengths, query_positions, slab_size, fresh_block):
    page_size = slab_size + fresh_block
    page_number = row_index // page_size
    offset = row_index - page_number * page_size
    page_count = lengths.shape[1]
    picker = page_number[None, :] == jnp.arange(page_count, dtype=jnp.int32)[:, None]
    live_length = jnp.sum(jnp.where(picker[None], lengths[:, :, None], 0), axis=1)
    in_cache = (offset < slab_size)[None, :] & (offset[None, :] < live_length)
    fresh_position = page_number * fresh_block + offset - slab_size
    in_fresh = (offset >= slab_size)[None, :] & (
        fresh_position[None, :] <= query_positions[:, None]
    )
    return in_cache[:, None, :] | in_fresh[None, :, :]


def per_device(
    queries,
    pages,
    cached_lengths,
    residual_in,
    out_weight,
    norm_gain,
    expert_ids,
    route_scores,
    expert_input,
    expert_output,
):
    requests, fresh_block, query_width = queries.shape
    local_heads = query_width // HEAD
    core_place = lax.axis_index("rep")
    page_place = lax.axis_index("ctx")
    rep_count = lax.axis_size("rep")
    page_size = pages.shape[1]
    slab_size = page_size - fresh_block
    own_positions = page_place * fresh_block + jnp.arange(fresh_block, dtype=jnp.int32)
    query_rows = queries.reshape(requests, fresh_block, local_heads, HEAD)
    start_state = (
        jnp.full((requests, fresh_block, local_heads), floor_value, jnp.float32),
        jnp.zeros((requests, fresh_block, local_heads), jnp.float32),
        jnp.zeros((requests, fresh_block, local_heads, HEAD), jnp.float32),
    )
    page_piece = lax.all_gather(pages, "ctx", axis=1, tiled=True)
    row_index = jnp.arange(page_piece.shape[1], dtype=jnp.int32)
    allowed = rows_mask(row_index, cached_lengths, own_positions, slab_size, fresh_block)
    peaks, totals, summed = merge_partials(
        start_state, attend_piece(query_rows, page_piece, allowed)
    )
    context = (
        (summed / totals[..., None])
        .astype(jnp.bfloat16)
        .reshape(requests, fresh_block, query_width)
    )
    projected = jnp.dot(
        context.reshape(requests * fresh_block, query_width),
        out_weight,
        preferred_element_type=jnp.float32,
    ).reshape(requests, fresh_block, -1)
    token_block = residual_in.shape[1]
    share_size = token_block // rep_count
    own_share = lax.psum_scatter(
        projected.astype(jnp.bfloat16), ("exp", "rep"), scatter_dimension=1, tiled=True
    ).astype(jnp.float32)
    own_residual = lax.dynamic_slice_in_dim(residual_in, core_place * share_size, share_size, 1)
    own_hidden = (own_residual.astype(jnp.float32) + own_share).astype(jnp.bfloat16)
    normed = lax.all_gather(normalize(own_hidden, norm_gain), "rep", axis=1, tiled=True)
    top_count = expert_ids.shape[2]
    expert_count = lax.axis_size("ctx") * lax.axis_size("exp")
    most_rows = max(2, (token_block * top_count + expert_count - 1) // expert_count)
    capacity = requests * most_rows
    model_width = normed.shape[2]
    token_count = requests * token_block
    flat_ids = expert_ids.reshape(-1)
    row_count = flat_ids.shape[0]
    chosen = (flat_ids[:, None] == jnp.arange(expert_count, dtype=jnp.int32)[None, :]).astype(
        jnp.int32
    )
    earlier_rows = jnp.cumsum(chosen, axis=0) - chosen
    slot_rank = jnp.sum(earlier_rows * chosen, axis=1)
    slot_index = flat_ids * capacity + slot_rank
    slot_onehot = (
        slot_index[:, None] == jnp.arange(expert_count * capacity, dtype=jnp.int32)[None, :]
    ).astype(jnp.bfloat16)
    token_onehot = (
        (jnp.arange(row_count, dtype=jnp.int32) // top_count)[:, None]
        == jnp.arange(token_count, dtype=jnp.int32)[None, :]
    ).astype(jnp.bfloat16)
    placement = jnp.dot(slot_onehot.T, token_onehot, preferred_element_type=jnp.float32).astype(
        jnp.bfloat16
    )
    outgoing = jnp.dot(
        placement, normed.reshape(token_count, model_width), preferred_element_type=jnp.float32
    )
    outgoing = outgoing.astype(jnp.bfloat16).reshape(expert_count, capacity, model_width)
    scores_sum = jnp.sum(route_scores, axis=2, keepdims=True)
    combine = (route_scores / scores_sum).astype(jnp.bfloat16).reshape(-1)
    gathering = jnp.dot(
        (token_onehot * combine[:, None]).T, slot_onehot, preferred_element_type=jnp.float32
    ).astype(jnp.bfloat16)
    gate_up = expert_input[0]
    down_weight = expert_output[0]
    arrived_rows = lax.all_to_all(outgoing, ("ctx", "exp"), split_axis=0, concat_axis=0, tiled=True)
    inner_rows = jnp.einsum(
        "nd,dgh->ngh",
        arrived_rows.reshape(-1, model_width),
        gate_up,
        preferred_element_type=jnp.float32,
    )
    activated = (jax.nn.silu(inner_rows[:, 0]) * inner_rows[:, 1]).astype(jnp.bfloat16)
    result = jnp.dot(activated, down_weight, preferred_element_type=jnp.float32).astype(
        jnp.bfloat16
    )
    returned = lax.all_to_all(
        result.reshape(arrived_rows.shape), ("ctx", "exp"), split_axis=0, concat_axis=0, tiled=True
    )
    mixture = jnp.dot(
        gathering,
        returned.reshape(expert_count * capacity, model_width),
        preferred_element_type=jnp.float32,
    )
    own_mixture = lax.psum_scatter(
        mixture.reshape(requests, token_block, model_width).astype(jnp.bfloat16),
        "rep",
        scatter_dimension=1,
        tiled=True,
    ).astype(jnp.float32)
    layer_out = (own_hidden.astype(jnp.float32) + own_mixture).astype(jnp.bfloat16)
    return (context, layer_out)


BF = jnp.bfloat16
F32 = jnp.float32
MESH = pl.DeviceIdType.MESH
VMEM_LIMIT = 60 * 1024 * 1024


def fused_kernel(
    ctx_count, exp_count, capacity,
    lengths, query, page, residual_in, gain_in, ids_in, scores_in, w_out, w_in, w_down,
    context_out, layer_out,
    lens, q_in, residual, gain, ids, scores,
    raw, raw_fresh, kv, kv_fresh, q_rows, peak, accum, wo, wi, wg, wu, wd,
    ids_all, scores_all, combine_all, place, gather,
    rs_full, rs_send, rs_recv, hidden, nz, x_send, x_recv, y_send, y_recv, mix_send, mix_recv,
    own_sem, in_sem, kv_left, kv_right, kv_recv, w_sem,
    ids_s, ids_r, sc_s, sc_r, rs_s, rs_r, nz_s, nz_r, dx_s, dx_r, ret_s, ret_r, mix_s, mix_r,
):
    ci = lax.axis_index("ctx")
    ei = lax.axis_index("exp")
    fresh = q_in.shape[0]
    heads = q_in.shape[1] // HEAD
    halves = raw.shape[1]
    half_rows = raw.shape[2]
    slab = halves * half_rows
    rows = residual.shape[0]
    width = residual.shape[1]
    top = ids.shape[0]
    scaling = HEAD ** (-0.5) * 1.4426950408889634

    def ctx_peer(k):
        return {"ctx": lax.rem(ci + k, ctx_count)}

    def exp_peer(k):
        return {"exp": lax.rem(ei + k, exp_count)}

    def remote(src, dst, ss, rs, where):
        return pltpu.make_async_remote_copy(
            src_ref=src, dst_ref=dst, send_sem=ss, recv_sem=rs, device_id=where, device_id_type=MESH
        )

    barrier = pltpu.get_barrier_semaphore()
    for k in range(1, ctx_count):
        pl.semaphore_signal(barrier, inc=1, device_id=ctx_peer(k), device_id_type=MESH)
    for k in range(1, exp_count):
        pl.semaphore_signal(barrier, inc=1, device_id=exp_peer(k), device_id_type=MESH)

    def page_piece(c):
        return page.at[pl.ds(c * half_rows, half_rows)] if c < halves else page.at[pl.ds(slab, fresh)]

    def raw_piece(p, c):
        return raw.at[p, c] if c < halves else raw_fresh.at[p]

    pieces_in_order = [halves] + list(range(halves))
    own_page = [pltpu.make_async_copy(page_piece(c), raw_piece(ci, c), own_sem.at[c]) for c in range(halves + 1)]
    for c in pieces_in_order:
        own_page[c].start()
    inputs = [
        pltpu.make_async_copy(src, dst, in_sem.at[n])
        for n, (src, dst) in enumerate(
            [(lengths, lens), (query, q_in), (residual_in, residual), (gain_in, gain), (ids_in, ids), (scores_in, scores)]
        )
    ]
    for c in inputs:
        c.start()
    copies_w = [
        pltpu.make_async_copy(w_out, wo, w_sem.at[0]),
        pltpu.make_async_copy(w_in, wi, w_sem.at[1]),
        pltpu.make_async_copy(w_down, wd, w_sem.at[2]),
    ]
    for n in (1, 0, 2):
        copies_w[n].start()

    kv[:, :, 2 * HEAD:] = jnp.ones(kv.shape[:2] + (HEAD,), BF)
    kv_fresh[:, :2 * HEAD] = jnp.zeros((kv_fresh.shape[0], 2 * HEAD), BF)
    kv_fresh[:, 2 * HEAD:] = jnp.ones((kv_fresh.shape[0], HEAD), BF)
    accum[...] = jnp.zeros_like(accum)
    peak[...] = jnp.full_like(peak, floor_value)
    pl.semaphore_wait(barrier, ctx_count + exp_count - 2)

    def send_right(p, c, src):
        dst = raw_piece(p, c) if isinstance(c, int) else raw.at[p, c]
        return remote(src, dst, kv_right.at[p, c], kv_recv.at[p, c], {"ctx": ci + 1})

    def send_left(p, c, src):
        dst = raw_piece(p, c) if isinstance(c, int) else raw.at[p, c]
        return remote(src, dst, kv_left.at[p, c], kv_recv.at[p, c], {"ctx": ci - 1})

    small = []
    for k in range(1, ctx_count):
        small.append(remote(ids_in, ids_all.at[ci], ids_s.at[k], ids_r.at[ci], ctx_peer(k)))
        small.append(remote(scores_in, scores_all.at[ci], sc_s.at[k], sc_r.at[ci], ctx_peer(k)))
    for c in small:
        c.start()

    for c in pieces_in_order:
        @pl.when(ci < ctx_count - 1)
        def _():
            send_right(ci, c, page_piece(c)).start()

        if c < halves:
            @pl.when(ci > 0)
            def _():
                send_left(ci, c, page_piece(c)).start()

    inputs[0].wait()
    inputs[1].wait()
    for h in range(heads):
        q_rows[h * fresh:(h + 1) * fresh, :] = q_in[:, h * HEAD:(h + 1) * HEAD]

    step = next(n for n in (4, 2, 1) if heads % n == 0)
    page_number = lax.broadcasted_iota(jnp.int32, (1, ctx_count), 1)
    slab_row = lax.broadcasted_iota(jnp.int32, (1, slab), 1).astype(F32)

    def split(p, c):
        both = pltpu.einshape("sgh->gsh", raw[p, c])
        at = pl.ds(pl.multiple_of(c * half_rows, half_rows), half_rows)
        kv[p, at, :HEAD] = both[0]
        kv[p, at, HEAD:2 * HEAD] = both[1]

    def split_fresh(p):
        both = pltpu.einshape("sgh->gsh", raw_fresh[p])
        at = pl.ds(pl.multiple_of(p * fresh, fresh), fresh)
        kv_fresh[at, :HEAD] = both[0]
        kv_fresh[at, HEAD:2 * HEAD] = both[1]

    def attend(source, bias):
        keys = source[:, :HEAD]
        values = source[:, HEAD:]
        count = keys.shape[0]
        for h in range(0, heads, step):
            sl = slice(h * fresh, (h + step) * fresh)
            s = lax.dot_general(
                q_rows[sl, :], keys, (((1,), (1,)), ((), ())), preferred_element_type=F32
            )
            s = (s.reshape(step, fresh, count) + bias[None]).reshape(step * fresh, count)
            old = peak[sl, :]
            now = jnp.maximum(old, jnp.max(s, axis=1, keepdims=True))
            w = jnp.exp2((s - now[:, :1]) * scaling)
            fade = jnp.exp2((old - now) * scaling)
            accum[sl, :] = accum[sl, :] * jnp.concatenate([fade, fade], 1) + jnp.dot(
                w.astype(BF), values, preferred_element_type=F32
            )
            peak[sl, :] = now

    def attend_page(p):
        live = jnp.sum(jnp.where(page_number == p, lens[...], 0).astype(F32), axis=1, keepdims=True)
        attend(kv.at[p], jnp.where(slab_row < live, 0.0, floor_value))

    def attend_fresh():
        count = kv_fresh.shape[0]
        position = lax.broadcasted_iota(jnp.int32, (fresh, count), 0) + ci * fresh
        attend(kv_fresh, jnp.where(lax.broadcasted_iota(jnp.int32, (fresh, count), 1) <= position, 0.0, floor_value))

    own_page[halves].wait()
    split_fresh(ci)
    for c in range(halves):
        own_page[c].wait()
        split(ci, c)
    attend_page(ci)

    steps = 2 * halves * (ctx_count - 1)
    depth = next(n for n in range(-(-width // (steps + 4)), width + 1) if width % n == 0 and n % 16 == 0)
    blocks = width // depth
    copies_w[1].wait()

    def unpack(i):
        at = pl.ds(pl.multiple_of(i * depth, depth), depth)
        block = pltpu.einshape("dgh->gdh", wi[at])
        wg[at, :] = block[0]
        wu[at, :] = block[1]

    ahead = max(0, blocks - steps)
    for i in range(ahead):
        unpack(i)

    for c in inputs[2:]:
        c.wait()
    ids_all[ci] = ids[...]
    scores_all[ci] = scores[...]
    for k in range(1, ctx_count):
        source = lax.rem(ci + k, ctx_count)
        remote(ids_in, ids_all.at[source], ids_s.at[k], ids_r.at[source], ctx_peer(k)).wait_recv()
        remote(scores_in, scores_all.at[source], sc_s.at[k], sc_r.at[source], ctx_peer(k)).wait_recv()
    for k in range(ctx_count):
        given = scores_all[k]
        combine_all[k] = (given / jnp.sum(given, axis=0, keepdims=True)).astype(BF).astype(F32)

    lanes = exp_count * capacity
    lane = lax.broadcasted_iota(jnp.int32, (lanes, rows), 0)
    wanted = ci * exp_count + lax.rem(ei + lane // capacity, exp_count)
    seat = (lane - lane // capacity * capacity).astype(F32)
    earlier = (
        lax.broadcasted_iota(jnp.int32, (rows, rows), 0)
        < lax.broadcasted_iota(jnp.int32, (rows, rows), 1)
    ).astype(F32)
    for k in range(ctx_count):
        chosen = jnp.zeros((lanes, rows), F32)
        portion = jnp.zeros((lanes, rows), F32)
        for j in range(top):
            hit = ids_all[k, j:j + 1, :] == wanted
            chosen = jnp.where(hit, 1.0, chosen)
            portion = jnp.where(hit, combine_all[k, j:j + 1, :], portion)
        rank = jnp.dot(chosen.astype(BF), earlier.astype(BF), preferred_element_type=F32)
        seated = (chosen > 0.5) & (rank == seat)
        place[k] = jnp.where(seated, 1.0, 0.0)
        gather[k] = jnp.where(seated, portion, 0.0)

    def pass_on(p, c):
        src = raw_piece(p, c) if isinstance(c, int) else raw.at[p, c]

        @pl.when((p < ci) & (ci < ctx_count - 1))
        def _():
            send_right(p, c, src).start()

        if not (isinstance(c, int) and c == halves):
            @pl.when((p > ci) & (ci > 0))
            def _():
                send_left(p, c, src).start()

    def arrival(i, carry):
        d = i // (2 * halves) + 1
        c = lax.rem(i // 2, halves)
        p = jnp.where(lax.rem(i, 2) == 0, ci - d, ci + d)

        @pl.when((p >= 0) & (p < ctx_count))
        def _():
            @pl.when((c == 0) & (p < ci))
            def _():
                send_right(p, halves, raw_fresh.at[p]).wait_recv()
                pass_on(p, halves)
                split_fresh(p)

            send_right(p, c, raw.at[p, c]).wait_recv()
            pass_on(p, c)
            split(p, c)

            @pl.when(c == halves - 1)
            def _():
                attend_page(p)

        @pl.when(i == jnp.maximum(ci - 1, 0) * 2 * halves)
        def _():
            attend_fresh()

        @pl.when(i + ahead < blocks)
        def _():
            unpack(i + ahead)

        return carry

    lax.fori_loop(0, steps, arrival, 0)

    for h in range(heads):
        sl = slice(h * fresh, (h + 1) * fresh)
        context_out[:, h * HEAD:(h + 1) * HEAD] = (accum[sl, :HEAD] / accum[sl, HEAD:]).astype(BF)

    copies_w[0].wait()

    pieces = 4
    piece = width // pieces
    own_share = []
    rs_copies = []
    for n in range(pieces):
        cols = slice(n * piece, (n + 1) * piece)
        part = jnp.dot(context_out[...], wo[:, cols], preferred_element_type=F32)
        rs_full[n] = part
        for k in range(1, exp_count):
            at = pl.ds(pl.multiple_of(lax.rem(ei + k, exp_count) * rows, rows), rows)
            rs_send[k, n] = rs_full[n, at, :].astype(BF)
            c = remote(rs_send.at[k, n], rs_recv.at[k, n], rs_s.at[k, n], rs_r.at[k, n], exp_peer(k))
            c.start()
            rs_copies.append(c)
    mine = pl.ds(pl.multiple_of(ei * rows, rows), rows)
    square = jnp.zeros((rows, 1), F32)
    for n in range(pieces):
        cols = slice(n * piece, (n + 1) * piece)
        share = rs_full[n, mine, :]
        for k in range(1, exp_count):
            rs_copies[n * (exp_count - 1) + k - 1].wait_recv()
            share = share + rs_recv[k, n].astype(F32)
        h = (residual[:, cols].astype(F32) + share).astype(BF)
        hidden[:, cols] = h
        wide = h.astype(F32)
        square = square + jnp.sum(wide * wide, axis=1, keepdims=True)
    inverse = lax.rsqrt(square / width + norm_epsilon)
    nz[ci] = (hidden[...].astype(F32) * inverse * gain[...]).astype(BF)

    last = ctx_count - 1
    middle = last / 2
    send_table, work_table = [], []
    for c in range(ctx_count):
        others = [p for p in range(ctx_count) if p != c]
        send_table.append(sorted(others, key=lambda p: (abs(p - c) % last, abs(p - middle))))
        work_table.append([c] + sorted(others, key=lambda p: ((abs(p - c) - 1) % (last - 1) if last > 1 else 0, abs(p - middle))))

    def lookup(table, n):
        value = jnp.int32(table[0][n])
        for c in range(1, ctx_count):
            value = jnp.where(ci == c, table[c][n], value)
        return value

    def nz_copy(p, n, where):
        return remote(nz.at[p], nz.at[p], nz_s.at[n], nz_r.at[p], {"ctx": where})

    nz_copies = []
    for n in range(last):
        c = nz_copy(ci, n, lookup(send_table, n))
        c.start()
        nz_copies.append(c)

    places = [lookup(work_table, n) for n in range(ctx_count)]

    def dx_copy(j, n):
        p = places[n]
        return remote(x_send.at[j, p], x_recv.at[j, p], dx_s.at[j, p], dx_r.at[j, p], exp_peer(j))

    def ret_copy(j, n):
        p = places[n]
        return remote(y_send.at[j, p], y_recv.at[j, p], ret_s.at[j, p], ret_r.at[j, p], exp_peer(exp_count - j))

    def mix_copy(n):
        p = places[n]
        return remote(mix_send.at[p], mix_recv.at[ci], mix_s.at[p], mix_r.at[ci], {"ctx": p})

    def dispatch(n):
        p = places[n]
        if n:
            nz_copy(p, 0, p).wait_recv()
        routed = jnp.dot(place[p].astype(BF), nz[p], preferred_element_type=F32)
        for j in list(range(1, exp_count)) + [0]:
            block = routed[j * capacity:(j + 1) * capacity].astype(BF)
            if j == 0:
                x_recv[0, p] = block
            else:
                x_send[j, p] = block
                dx_copy(j, n).start()

    def experts(n):
        p = places[n]
        for j in range(1, exp_count):
            dx_copy(j, n).wait_recv()
        x = jnp.concatenate([x_recv[j, p].astype(F32) for j in range(exp_count)], 0).astype(BF)
        gate = jnp.dot(x, wg[...], preferred_element_type=F32)
        up = jnp.dot(x, wu[...], preferred_element_type=F32)
        act = (gate / (1.0 + jnp.exp(-gate)) * up).astype(BF)
        result = jnp.dot(act, wd[...], preferred_element_type=F32)
        for j in list(range(1, exp_count)) + [0]:
            block = result[j * capacity:(j + 1) * capacity].astype(BF)
            if j == 0:
                y_recv[0, p] = block
            else:
                y_send[j, p] = block
                ret_copy(j, n).start()

    def mixing(n):
        p = places[n]
        for j in range(1, exp_count):
            ret_copy(j, n).wait_recv()
        rows_p = jnp.concatenate([y_recv[j, p].astype(F32) for j in range(exp_count)], 0).astype(BF)
        mixed = lax.dot_general(
            gather[p].astype(BF), rows_p, (((0,), (0,)), ((), ())), preferred_element_type=F32
        )
        if n == 0:
            return mixed
        mix_send[p] = mixed.astype(BF)
        mix_copy(n).start()

    dispatch(0)
    for n in range(1, ctx_count):
        dispatch(n)
        if n == 1:
            copies_w[2].wait()
        experts(n - 1)
        if n > 2:
            mixing(n - 2)
    experts(ctx_count - 1)
    for n in range(max(1, ctx_count - 2), ctx_count):
        mixing(n)
    out = hidden[...].astype(F32) + mixing(0)
    for n in range(1, ctx_count):
        p = places[n]
        remote(mix_send.at[p], mix_recv.at[p], mix_s.at[p], mix_r.at[p], {"ctx": p}).wait_recv()
        out = out + mix_recv[p].astype(F32)
    layer_out[...] = out.astype(BF)

    for c in rs_copies + nz_copies + small:
        c.wait_send()
    for n in range(ctx_count):
        for j in range(1, exp_count):
            dx_copy(j, n).wait_send()
            ret_copy(j, n).wait_send()
        if n:
            mix_copy(n).wait_send()

    for c in pieces_in_order:
        @pl.when(ci < ctx_count - 1)
        def _():
            send_right(ci, c, page_piece(c)).wait_send()

        if c < halves:
            @pl.when(ci > 0)
            def _():
                send_left(ci, c, page_piece(c)).wait_send()

    def drain(p, carry):
        for c in pieces_in_order:
            @pl.when((p < ci) & (ci < ctx_count - 1))
            def _():
                send_right(p, c, raw_piece(p, c)).wait_send()

            if c < halves:
                @pl.when((p > ci) & (ci > 0))
                def _():
                    send_left(p, c, raw_piece(p, c)).wait_send()

        return carry

    lax.fori_loop(0, ctx_count, drain, 0)


def fused_device(
    ctx_count, exp_count, queries, pages, cached_lengths, residual_in, out_weight, norm_gain,
    expert_ids, route_scores, expert_input, expert_output,
):
    fresh, query_width = queries.shape[1:]
    page_size = pages.shape[1]
    slab = page_size - fresh
    rows, width = residual_in.shape[1:]
    top = expert_ids.shape[2]
    hidden_width = expert_input.shape[3]
    experts = ctx_count * exp_count
    capacity = max(2, -(-rows * top // experts))
    stacked = query_width // HEAD * fresh
    vm = pl.BlockSpec(memory_space=pltpu.VMEM)
    hbm = pl.BlockSpec(memory_space=pl.ANY)
    dma = pltpu.SemaphoreType.DMA
    V = pltpu.VMEM
    lanes = exp_count * capacity
    pieces = 4
    halves = 2 if slab % 32 == 0 else 1
    context, layer_out = pl.pallas_call(
        functools.partial(fused_kernel, ctx_count, exp_count, capacity),
        out_shape=(V((fresh, query_width), BF), V((rows, width), BF)),
        in_specs=[hbm] * 10,
        out_specs=(vm, vm),
        scratch_shapes=[
            V((1, ctx_count), jnp.int32),
            V((fresh, query_width), BF),
            V((rows, width), BF),
            V((1, width), F32),
            V((top, rows), jnp.int32),
            V((top, rows), F32),
            V((ctx_count, halves, slab // halves) + pages.shape[2:], BF),
            V((ctx_count, fresh) + pages.shape[2:], BF),
            V((ctx_count, slab, 3 * HEAD), BF),
            V((ctx_count * fresh, 3 * HEAD), BF),
            V((stacked, HEAD), BF),
            V((stacked, HEAD), F32),
            V((stacked, 2 * HEAD), F32),
            V(out_weight.shape, BF),
            V(expert_input.shape[1:], BF),
            V((width, hidden_width), BF),
            V((width, hidden_width), BF),
            V(expert_output.shape[1:], BF),
            V((ctx_count, top, rows), jnp.int32),
            V((ctx_count, top, rows), F32),
            V((ctx_count, top, rows), F32),
            V((ctx_count, lanes, rows), F32),
            V((ctx_count, lanes, rows), F32),
            V((pieces, fresh, width // pieces), F32),
            V((exp_count, pieces, rows, width // pieces), BF),
            V((exp_count, pieces, rows, width // pieces), BF),
            V((rows, width), BF),
            V((ctx_count, rows, width), BF),
            V((exp_count, ctx_count, capacity, width), BF),
            V((exp_count, ctx_count, capacity, width), BF),
            V((exp_count, ctx_count, capacity, width), BF),
            V((exp_count, ctx_count, capacity, width), BF),
            V((ctx_count, rows, width), BF),
            V((ctx_count, rows, width), BF),
            dma((halves + 1,)), dma((6,)),
            dma((ctx_count, halves + 1)), dma((ctx_count, halves + 1)), dma((ctx_count, halves + 1)), dma((3,)),
            dma((ctx_count,)), dma((ctx_count,)), dma((ctx_count,)), dma((ctx_count,)),
            dma((exp_count, pieces)), dma((exp_count, pieces)),
            dma((ctx_count,)), dma((ctx_count,)),
            dma((exp_count, ctx_count)), dma((exp_count, ctx_count)),
            dma((exp_count, ctx_count)), dma((exp_count, ctx_count)),
            dma((ctx_count,)), dma((ctx_count,)),
        ],
        compiler_params=pltpu.CompilerParams(
            collective_id=0, has_side_effects=True, vmem_limit_bytes=VMEM_LIMIT
        ),
    )(
        cached_lengths, queries[0], pages[0], residual_in[0], norm_gain.reshape(1, width),
        expert_ids[0].T, route_scores[0].T, out_weight, expert_input[0], expert_output[0],
    )
    return context[None], layer_out[None]


def fused_fits(mesh):
    return mesh.shape["rep"] == 1 and mesh.shape["ctx"] <= 8


def solution(mesh):
    in_specs = (
        P("groups", "ctx", ("exp", "rep")),
        P("groups", "ctx", None, "exp"),
        P("groups", None),
        P("groups", ("ctx", "exp"), None),
        P(("exp", "rep"), None),
        P(),
        P("groups", ("ctx", "exp"), None),
        P("groups", ("ctx", "exp"), None),
        P(("ctx", "exp"), None, None, "rep"),
        P(("ctx", "exp"), "rep", None),
    )
    out_specs = (P("groups", "ctx", ("exp", "rep")), P("groups", ("ctx", "exp", "rep"), None))
    body = per_device
    if fused_fits(mesh):
        body = functools.partial(fused_device, mesh.shape["ctx"], mesh.shape["exp"])
    return jax.shard_map(
        body, mesh=mesh, in_specs=in_specs, out_specs=out_specs, check_vma=False
    )
```

```python
import functools

import jax
import jax.numpy as jnp
from jax import lax
from jax.experimental import pallas as pl
from jax.experimental.pallas import tpu as pltpu
from jax.sharding import PartitionSpec as P

HEAD = 128


floor_value = -1e30
norm_epsilon = 1e-06


def normalize(hidden, norm_gain):
    widened = hidden.astype(jnp.float32)
    mean_square = jnp.mean(widened * widened, axis=-1, keepdims=True)
    return (widened * lax.rsqrt(mean_square + norm_epsilon) * norm_gain).astype(jnp.bfloat16)


def attend_piece(query_rows, page_rows, allowed):
    scaling = query_rows.shape[-1] ** (-0.5)
    scores = (
        jnp.einsum(
            "rqhe,rke->rqhk", query_rows, page_rows[:, :, 0], preferred_element_type=jnp.float32
        )
        * scaling
    )
    permitted = allowed[:, :, None, :]
    masked = jnp.where(permitted, scores, floor_value)
    peaks = jnp.max(masked, axis=-1)
    weights = jnp.where(permitted, jnp.exp(masked - peaks[..., None]), 0.0)
    totals = jnp.sum(weights, axis=-1)
    summed = jnp.einsum(
        "rqhk,rke->rqhe",
        weights.astype(jnp.bfloat16),
        page_rows[:, :, 1],
        preferred_element_type=jnp.float32,
    )
    return (peaks, totals, summed)


def merge_partials(earlier, later):
    peaks = jnp.maximum(earlier[0], later[0])
    later_scale = jnp.exp(later[0] - peaks)
    totals = later[1] * later_scale
    summed = later[2] * later_scale[..., None]
    return (peaks, totals, summed)


def rows_mask(row_index, lengths, query_positions, slab_size, fresh_block):
    page_size = slab_size + fresh_block
    page_number = row_index // page_size
    offset = row_index - page_number * page_size
    page_count = lengths.shape[1]
    picker = page_number[None, :] == jnp.arange(page_count, dtype=jnp.int32)[:, None]
    live_length = jnp.sum(jnp.where(picker[None], lengths[:, :, None], 0), axis=1)
    in_cache = (offset < slab_size)[None, :] & (offset[None, :] < live_length)
    fresh_position = page_number * fresh_block + offset - slab_size
    in_fresh = (offset >= slab_size)[None, :] & (
        fresh_position[None, :] <= query_positions[:, None]
    )
    return in_cache[:, None, :] | in_fresh[None, :, :]


def per_device(
    queries,
    pages,
    cached_lengths,
    residual_in,
    out_weight,
    norm_gain,
    expert_ids,
    route_scores,
    expert_input,
    expert_output,
):
    requests, fresh_block, query_width = queries.shape
    local_heads = query_width // HEAD
    core_place = lax.axis_index("rep")
    page_place = lax.axis_index("ctx")
    rep_count = lax.axis_size("rep")
    page_size = pages.shape[1]
    slab_size = page_size - fresh_block
    own_positions = page_place * fresh_block + jnp.arange(fresh_block, dtype=jnp.int32)
    query_rows = queries.reshape(requests, fresh_block, local_heads, HEAD)
    start_state = (
        jnp.full((requests, fresh_block, local_heads), floor_value, jnp.float32),
        jnp.zeros((requests, fresh_block, local_heads), jnp.float32),
        jnp.zeros((requests, fresh_block, local_heads, HEAD), jnp.float32),
    )
    page_piece = lax.all_gather(pages, "ctx", axis=1, tiled=True)
    row_index = jnp.arange(page_piece.shape[1], dtype=jnp.int32)
    allowed = rows_mask(row_index, cached_lengths, own_positions, slab_size, fresh_block)
    peaks, totals, summed = merge_partials(
        start_state, attend_piece(query_rows, page_piece, allowed)
    )
    context = (
        (summed / totals[..., None])
        .astype(jnp.bfloat16)
        .reshape(requests, fresh_block, query_width)
    )
    projected = jnp.dot(
        context.reshape(requests * fresh_block, query_width),
        out_weight,
        preferred_element_type=jnp.float32,
    ).reshape(requests, fresh_block, -1)
    token_block = residual_in.shape[1]
    share_size = token_block // rep_count
    own_share = lax.psum_scatter(
        projected.astype(jnp.bfloat16), ("exp", "rep"), scatter_dimension=1, tiled=True
    ).astype(jnp.float32)
    own_residual = lax.dynamic_slice_in_dim(residual_in, core_place * share_size, share_size, 1)
    own_hidden = (own_residual.astype(jnp.float32) + own_share).astype(jnp.bfloat16)
    normed = lax.all_gather(normalize(own_hidden, norm_gain), "rep", axis=1, tiled=True)
    top_count = expert_ids.shape[2]
    expert_count = lax.axis_size("ctx") * lax.axis_size("exp")
    most_rows = max(2, (token_block * top_count + expert_count - 1) // expert_count)
    capacity = requests * most_rows
    model_width = normed.shape[2]
    token_count = requests * token_block
    flat_ids = expert_ids.reshape(-1)
    row_count = flat_ids.shape[0]
    chosen = (flat_ids[:, None] == jnp.arange(expert_count, dtype=jnp.int32)[None, :]).astype(
        jnp.int32
    )
    earlier_rows = jnp.cumsum(chosen, axis=0) - chosen
    slot_rank = jnp.sum(earlier_rows * chosen, axis=1)
    slot_index = flat_ids * capacity + slot_rank
    slot_onehot = (
        slot_index[:, None] == jnp.arange(expert_count * capacity, dtype=jnp.int32)[None, :]
    ).astype(jnp.bfloat16)
    token_onehot = (
        (jnp.arange(row_count, dtype=jnp.int32) // top_count)[:, None]
        == jnp.arange(token_count, dtype=jnp.int32)[None, :]
    ).astype(jnp.bfloat16)
    placement = jnp.dot(slot_onehot.T, token_onehot, preferred_element_type=jnp.float32).astype(
        jnp.bfloat16
    )
    outgoing = jnp.dot(
        placement, normed.reshape(token_count, model_width), preferred_element_type=jnp.float32
    )
    outgoing = outgoing.astype(jnp.bfloat16).reshape(expert_count, capacity, model_width)
    scores_sum = jnp.sum(route_scores, axis=2, keepdims=True)
    combine = (route_scores / scores_sum).astype(jnp.bfloat16).reshape(-1)
    gathering = jnp.dot(
        (token_onehot * combine[:, None]).T, slot_onehot, preferred_element_type=jnp.float32
    ).astype(jnp.bfloat16)
    gate_up = expert_input[0]
    down_weight = expert_output[0]
    arrived_rows = lax.all_to_all(outgoing, ("ctx", "exp"), split_axis=0, concat_axis=0, tiled=True)
    inner_rows = jnp.einsum(
        "nd,dgh->ngh",
        arrived_rows.reshape(-1, model_width),
        gate_up,
        preferred_element_type=jnp.float32,
    )
    activated = (jax.nn.silu(inner_rows[:, 0]) * inner_rows[:, 1]).astype(jnp.bfloat16)
    result = jnp.dot(activated, down_weight, preferred_element_type=jnp.float32).astype(
        jnp.bfloat16
    )
    returned = lax.all_to_all(
        result.reshape(arrived_rows.shape), ("ctx", "exp"), split_axis=0, concat_axis=0, tiled=True
    )
    mixture = jnp.dot(
        gathering,
        returned.reshape(expert_count * capacity, model_width),
        preferred_element_type=jnp.float32,
    )
    own_mixture = lax.psum_scatter(
        mixture.reshape(requests, token_block, model_width).astype(jnp.bfloat16),
        "rep",
        scatter_dimension=1,
        tiled=True,
    ).astype(jnp.float32)
    layer_out = (own_hidden.astype(jnp.float32) + own_mixture).astype(jnp.bfloat16)
    return (context, layer_out)


BF = jnp.bfloat16
F32 = jnp.float32
MESH = pl.DeviceIdType.MESH
VMEM_LIMIT = 60 * 1024 * 1024


def fused_kernel(
    ctx_count, exp_count, capacity,
    lengths, query, page, residual_in, gain_in, ids_in, scores_in, w_out, w_in, w_down,
    context_out, layer_out,
    lens, q_in, residual, gain, ids, scores,
    raw, kv, kv_fresh, q_rows, peak, accum, part_send, part_recv, level_send, level_recv,
    wo, wi, wg, wu, wd,
    ids_all, scores_all, combine_all, place, gather,
    rs_full, rs_send, rs_recv, hidden, nz, x_send, x_recv, y_send, y_recv, mix_send, mix_recv,
    own_sem, in_sem, kv_send, kv_recv, w_sem, q_sem, part_sem,
    ids_s, ids_r, sc_s, sc_r, rs_s, rs_r, nz_s, nz_r, dx_s, dx_r, ret_s, ret_r, mix_s, mix_r,
):
    ci = lax.axis_index("ctx")
    ei = lax.axis_index("exp")
    fresh = q_in.shape[1]
    heads = q_in.shape[2] // HEAD
    slab = kv.shape[1]
    halves = 2 if slab % 32 == 0 else 1
    half_rows = slab // halves
    rows = residual.shape[0]
    width = residual.shape[1]
    top = ids.shape[0]
    stacked = q_rows.shape[1]
    scaling = HEAD ** (-0.5) * 1.4426950408889634

    last = ctx_count - 1
    edge = (ci == 0) | (ci == last)
    inner = (ci > 0) & (ci < last)
    near_edge = jnp.where(ci < 2, 0, last)
    across = last - ci
    far_edge = last - near_edge
    beside_edge = jnp.where(ci == 0, 1, last - 1)

    def ctx_peer(k):
        return {"ctx": lax.rem(ci + k, ctx_count)}

    def exp_peer(k):
        return {"exp": lax.rem(ei + k, exp_count)}

    def remote(src, dst, ss, rs, where):
        return pltpu.make_async_remote_copy(
            src_ref=src, dst_ref=dst, send_sem=ss, recv_sem=rs, device_id=where, device_id_type=MESH
        )

    barrier = pltpu.get_barrier_semaphore()
    for k in range(1, ctx_count):
        pl.semaphore_signal(barrier, inc=1, device_id=ctx_peer(k), device_id_type=MESH)
    for k in range(1, exp_count):
        pl.semaphore_signal(barrier, inc=1, device_id=exp_peer(k), device_id_type=MESH)

    own_page = pltpu.make_async_copy(page, raw.at[ci], own_sem.at[0])
    own_page.start()
    inputs = [
        pltpu.make_async_copy(src, dst, in_sem.at[n])
        for n, (src, dst) in enumerate(
            [(lengths, lens), (query, q_in.at[0]), (residual_in, residual), (gain_in, gain), (ids_in, ids), (scores_in, scores)]
        )
    ]
    for c in inputs:
        c.start()
    copies_w = [
        pltpu.make_async_copy(w_out, wo, w_sem.at[0]),
        pltpu.make_async_copy(w_in, wi, w_sem.at[1]),
        pltpu.make_async_copy(w_down, wd, w_sem.at[2]),
    ]
    for n in (1, 0, 2):
        copies_w[n].start()

    kv[:, :, 2 * HEAD:] = jnp.ones(kv.shape[:2] + (HEAD,), BF)
    kv_fresh[:, :2 * HEAD] = jnp.zeros((kv_fresh.shape[0], 2 * HEAD), BF)
    kv_fresh[:, 2 * HEAD:] = jnp.ones((kv_fresh.shape[0], HEAD), BF)
    accum[...] = jnp.zeros_like(accum)
    peak[...] = jnp.full_like(peak, floor_value)
    pl.semaphore_wait(barrier, ctx_count + exp_count - 2)

    small = []
    for k in range(1, ctx_count):
        small.append(remote(ids_in, ids_all.at[ci], ids_s.at[0], ids_r.at[0], ctx_peer(k)))
        small.append(remote(scores_in, scores_all.at[ci], sc_s.at[0], sc_r.at[0], ctx_peer(k)))
    for c in small:
        c.start()

    def rows_of(c):
        return pl.ds(c * half_rows, half_rows) if c < halves else pl.ds(slab, fresh)

    def piece(p, c, src, sem, step):
        return remote(src.at[rows_of(c)], raw.at[p, rows_of(c)], kv_send.at[sem], kv_recv.at[p, c], {"ctx": ci + step})

    order_right = [halves] + list(range(halves))
    order_left = list(range(halves))

    @pl.when(ci < last)
    def _():
        for c in order_right:
            piece(ci, c, page, 0, 1).start()

    @pl.when(ci > 0)
    def _():
        for c in order_left:
            piece(ci, c, page, 1, -1).start()

    def query_copy(where):
        return remote(query, q_in.at[1], q_sem.at[0], q_sem.at[1], {"ctx": where})

    @pl.when(edge)
    def _():
        query_copy(beside_edge).start()

    def stage_queries(n):
        for h in range(heads):
            q_rows[n, h * fresh:(h + 1) * fresh, :] = q_in[n, :, h * HEAD:(h + 1) * HEAD]

    inputs[0].wait()
    inputs[1].wait()
    stage_queries(0)

    step = next(n for n in (4, 2, 1) if heads % n == 0)
    page_number = lax.broadcasted_iota(jnp.int32, (1, ctx_count), 1)
    slab_row = lax.broadcasted_iota(jnp.int32, (1, slab), 1).astype(F32)

    def split(p, c):
        both = pltpu.einshape("sgh->gsh", raw[p, rows_of(c)])
        if c < halves:
            kv[p, rows_of(c), :HEAD] = both[0]
            kv[p, rows_of(c), HEAD:2 * HEAD] = both[1]
        else:
            at = pl.ds(pl.multiple_of(p * fresh, fresh), fresh)
            kv_fresh[at, :HEAD] = both[0]
            kv_fresh[at, HEAD:2 * HEAD] = both[1]

    def attend(n, source, bias):
        keys = source[:, :HEAD]
        values = source[:, HEAD:]
        count = keys.shape[0]
        for h in range(0, heads, step):
            sl = slice(h * fresh, (h + step) * fresh)
            s = lax.dot_general(
                q_rows[n, sl, :], keys, (((1,), (1,)), ((), ())), preferred_element_type=F32
            )
            s = (s.reshape(step, fresh, count) + bias[None]).reshape(step * fresh, count)
            old = peak[n, sl, :]
            now = jnp.maximum(old, jnp.max(s, axis=1, keepdims=True))
            w = jnp.exp2((s - now[:, :1]) * scaling)
            fade = jnp.exp2((old - now) * scaling)
            accum[n, sl, :] = accum[n, sl, :] * jnp.concatenate([fade, fade], 1) + jnp.dot(
                w.astype(BF), values, preferred_element_type=F32
            )
            peak[n, sl, :] = now

    def attend_page(n, p):
        live = jnp.sum(jnp.where(page_number == p, lens[...], 0).astype(F32), axis=1, keepdims=True)
        attend(n, kv.at[p], jnp.where(slab_row < live, 0.0, floor_value))

    def attend_fresh(n, home, first, count):
        count *= fresh
        at = pl.ds(pl.multiple_of(first * fresh, fresh), count)
        row = lax.broadcasted_iota(jnp.int32, (fresh, count), 1) + first * fresh
        position = lax.broadcasted_iota(jnp.int32, (fresh, count), 0) + home * fresh
        attend(n, kv_fresh.at[at], jnp.where(row <= position, 0.0, floor_value))

    own_page.wait()
    for c in order_right:
        split(ci, c)
    attend_page(0, ci)

    depth = next(n for n in (256, 128, 64, 32, 16) if width % n == 0)
    copies_w[1].wait()

    def unpack(i, carry):
        at = pl.ds(pl.multiple_of(i * depth, depth), depth)
        block = pltpu.einshape("dgh->gdh", wi[at])
        wg[at, :] = block[0]
        wu[at, :] = block[1]
        return carry

    lax.fori_loop(0, width // depth, unpack, 0)

    for c in inputs[2:]:
        c.wait()
    ids_all[ci] = ids[...]
    scores_all[ci] = scores[...]

    def route():
        others = pl.ds(0, last)
        remote(ids_all.at[others], ids_all.at[others], ids_s.at[0], ids_r.at[0], ctx_peer(1)).wait_recv()
        remote(scores_all.at[others], scores_all.at[others], sc_s.at[0], sc_r.at[0], ctx_peer(1)).wait_recv()
        lanes = exp_count * capacity
        lane = lax.broadcasted_iota(jnp.int32, (lanes, rows), 0)
        wanted = ci * exp_count + lax.rem(ei + lane // capacity, exp_count)
        seat = (lane - lane // capacity * capacity).astype(F32)
        earlier = (
            lax.broadcasted_iota(jnp.int32, (rows, rows), 0)
            < lax.broadcasted_iota(jnp.int32, (rows, rows), 1)
        ).astype(F32)
        for k in range(ctx_count):
            given = scores_all[k]
            combine_all[k] = (given / jnp.sum(given, axis=0, keepdims=True)).astype(BF).astype(F32)
        for k in range(ctx_count):
            chosen = jnp.zeros((lanes, rows), F32)
            portion = jnp.zeros((lanes, rows), F32)
            for j in range(top):
                hit = ids_all[k, j:j + 1, :] == wanted
                chosen = jnp.where(hit, 1.0, chosen)
                portion = jnp.where(hit, combine_all[k, j:j + 1, :], portion)
            rank = jnp.dot(chosen.astype(BF), earlier.astype(BF), preferred_element_type=F32)
            seated = (chosen > 0.5) & (rank == seat)
            place[k] = jnp.where(seated, 1.0, 0.0)
            gather[k] = jnp.where(seated, portion, 0.0)

    def arrive(p, c):
        piece(p, c, raw.at[p], 0, 1).wait_recv()

    def pass_on(c):
        @pl.when(ci < across)
        def _():
            piece(near_edge, c, raw.at[near_edge], 2, 1).start()

        if c < halves:
            @pl.when(ci > across)
            def _():
                piece(near_edge, c, raw.at[near_edge], 2, -1).start()

    def arrive_fresh(p):
        arrive(p, halves)
        split(p, halves)

    block_rows = stacked // level_send.shape[0]

    def part_copies(where):
        return (
            remote(part_send, part_recv, part_sem.at[0], part_sem.at[1], {"ctx": where}),
            remote(level_send, level_recv, part_sem.at[2], part_sem.at[3], {"ctx": where}),
        )

    @pl.when(inner)
    def _():
        @pl.when(ci < across)
        def _():
            arrive(near_edge, halves)
            pass_on(halves)
            split(near_edge, halves)

        @pl.when(ci > across)
        def _():
            arrive_fresh(across)

        for c in range(halves):
            arrive(near_edge, c)
            pass_on(c)
            split(near_edge, c)
            if c == 0:
                route()
            arrive(across, c)
            split(across, c)
        attend_page(0, near_edge)
        attend_page(0, across)
        query_copy(ci).wait_recv()
        stage_queries(1)
        attend_page(1, across)

        @pl.when(ci > across)
        def _():
            arrive_fresh(far_edge)
            attend_fresh(1, near_edge, 0, ctx_count // 2)

        attend_fresh(0, ci, 0, ctx_count)
        for c in range(halves):
            arrive(far_edge, c)
            split(far_edge, c)
        attend_page(1, far_edge)
        for b in range(stacked // block_rows):
            sl = slice(b * block_rows, (b + 1) * block_rows)
            whole = accum[1, sl, HEAD:]
            part_send[sl, :] = (accum[1, sl, :HEAD] / whole).astype(BF)
            level = peak[1, sl, :] * scaling + jnp.log(whole) * 1.4426950408889634
            level_send[b:b + 1, :] = jnp.transpose(level)[:1, :]
        for c in part_copies(near_edge):
            c.start()
        attend_page(0, far_edge)
        for h in range(heads):
            sl = slice(h * fresh, (h + 1) * fresh)
            context_out[:, h * HEAD:(h + 1) * HEAD] = (accum[0, sl, :HEAD] / accum[0, sl, HEAD:]).astype(BF)

    @pl.when(edge)
    def _():
        route()

        @pl.when(ci > 0)
        def _():
            arrive_fresh(beside_edge)

        attend_fresh(0, ci, jnp.where(ci == 0, 0, ctx_count // 2), ctx_count // 2)
        for c in range(halves):
            arrive(beside_edge, c)
            split(beside_edge, c)
        attend_page(0, beside_edge)
        for c in part_copies(ci):
            c.wait_recv()
        per = block_rows // fresh
        for b in range(stacked // block_rows):
            sl = slice(b * block_rows, (b + 1) * block_rows)
            theirs = jnp.transpose(jnp.broadcast_to(level_recv[b:b + 1, :], (HEAD, block_rows)))
            ours = peak[0, sl, :] * scaling
            level = jnp.maximum(ours, theirs)
            fade = jnp.exp2(ours - level)
            share = jnp.exp2(theirs - level)
            merged = (accum[0, sl, :HEAD] * fade + part_recv[sl, :].astype(F32) * share) / (
                accum[0, sl, HEAD:] * fade + share
            )
            for h in range(per):
                at = b * per + h
                context_out[:, at * HEAD:(at + 1) * HEAD] = merged[h * fresh:(h + 1) * fresh, :].astype(BF)

    copies_w[0].wait()

    pieces = 4
    piece_width = width // pieces
    senders = pl.ds(1, exp_count - 1)
    for n in range(pieces):
        cols = slice(n * piece_width, (n + 1) * piece_width)
        part = jnp.dot(context_out[...], wo[:, cols], preferred_element_type=F32)
        rs_full[n] = part
        for k in range(1, exp_count):
            at = pl.ds(pl.multiple_of(lax.rem(ei + k, exp_count) * rows, rows), rows)
            rs_send[k, n] = rs_full[n, at, :].astype(BF)
            remote(rs_send.at[k, n], rs_recv.at[k, n], rs_s.at[0], rs_r.at[n], exp_peer(k)).start()
    mine = pl.ds(pl.multiple_of(ei * rows, rows), rows)
    square = jnp.zeros((rows, 1), F32)
    for n in range(pieces):
        cols = slice(n * piece_width, (n + 1) * piece_width)
        share = rs_full[n, mine, :]
        remote(rs_send.at[senders, n], rs_recv.at[senders, n], rs_s.at[0], rs_r.at[n], exp_peer(1)).wait_recv()
        for k in range(1, exp_count):
            share = share + rs_recv[k, n].astype(F32)
        h = (residual[:, cols].astype(F32) + share).astype(BF)
        hidden[:, cols] = h
        wide = h.astype(F32)
        square = square + jnp.sum(wide * wide, axis=1, keepdims=True)
    inverse = lax.rsqrt(square / width + norm_epsilon)
    nz[ci] = (hidden[...].astype(F32) * inverse * gain[...]).astype(BF)

    middle = last / 2
    send_table, work_table = [], []
    for c in range(ctx_count):
        others = [p for p in range(ctx_count) if p != c]
        send_table.append(sorted(others, key=lambda p: (abs(p - c) % last, abs(p - middle))))
        work_table.append([c] + sorted(others, key=lambda p: ((abs(p - c) - 1) % (last - 1) if last > 1 else 0, abs(p - middle))))

    def lookup(table, n):
        value = jnp.int32(table[0][n])
        for c in range(1, ctx_count):
            value = jnp.where(ci == c, table[c][n], value)
        return value

    def nz_copy(p, where):
        return remote(nz.at[p], nz.at[p], nz_s.at[0], nz_r.at[p], {"ctx": where})

    for n in range(last):
        nz_copy(ci, lookup(send_table, n)).start()

    places = [lookup(work_table, n) for n in range(ctx_count)]

    def dx_copy(j, n):
        p = places[n]
        return remote(x_send.at[j, p], x_recv.at[j, p], dx_s.at[0], dx_r.at[p], exp_peer(1 if j is senders else j))

    def ret_copy(j, n):
        p = places[n]
        return remote(y_send.at[j, p], y_recv.at[j, p], ret_s.at[0], ret_r.at[p], exp_peer(1 if j is senders else exp_count - j))

    def mix_copy(n):
        p = places[n]
        return remote(mix_send.at[p], mix_recv.at[ci], mix_s.at[0], mix_r.at[ci], {"ctx": p})

    def dispatch(n):
        p = places[n]
        if n:
            nz_copy(p, p).wait_recv()
        routed = jnp.dot(place[p].astype(BF), nz[p], preferred_element_type=F32)
        for j in list(range(1, exp_count)) + [0]:
            block = routed[j * capacity:(j + 1) * capacity].astype(BF)
            if j == 0:
                x_recv[0, p] = block
            else:
                x_send[j, p] = block
                dx_copy(j, n).start()

    def experts(n):
        p = places[n]
        dx_copy(senders, n).wait_recv()
        x = jnp.concatenate([x_recv[j, p].astype(F32) for j in range(exp_count)], 0).astype(BF)
        gate = jnp.dot(x, wg[...], preferred_element_type=F32)
        up = jnp.dot(x, wu[...], preferred_element_type=F32)
        act = (gate / (1.0 + jnp.exp(-gate)) * up).astype(BF)
        result = jnp.dot(act, wd[...], preferred_element_type=F32)
        for j in list(range(1, exp_count)) + [0]:
            block = result[j * capacity:(j + 1) * capacity].astype(BF)
            if j == 0:
                y_recv[0, p] = block
            else:
                y_send[j, p] = block
                ret_copy(j, n).start()

    def mixing(n):
        p = places[n]
        ret_copy(senders, n).wait_recv()
        rows_p = jnp.concatenate([y_recv[j, p].astype(F32) for j in range(exp_count)], 0).astype(BF)
        mixed = lax.dot_general(
            gather[p].astype(BF), rows_p, (((0,), (0,)), ((), ())), preferred_element_type=F32
        )
        if n == 0:
            return mixed
        mix_send[p] = mixed.astype(BF)
        mix_copy(n).start()

    dispatch(0)
    for n in range(1, ctx_count):
        dispatch(n)
        if n == 1:
            copies_w[2].wait()
        experts(n - 1)
        if n > 2:
            mixing(n - 2)
    experts(ctx_count - 1)
    for n in range(max(1, ctx_count - 2), ctx_count):
        mixing(n)
    out = hidden[...].astype(F32) + mixing(0)
    for n in range(1, ctx_count):
        p = places[n]
        remote(mix_send.at[p], mix_recv.at[p], mix_s.at[0], mix_r.at[p], {"ctx": p}).wait_recv()
        out = out + mix_recv[p].astype(F32)
    layer_out[...] = out.astype(BF)

    others = pl.ds(0, last)
    for src, dst, sem in [
        (ids_all.at[others], ids_all.at[others], ids_s), (scores_all.at[others], scores_all.at[others], sc_s),
        (nz.at[others], nz.at[others], nz_s), (mix_send.at[others], mix_recv.at[others], mix_s),
    ]:
        remote(src, dst, sem.at[0], mix_r.at[0], ctx_peer(1)).wait_send()
    for src, dst, sem in [
        (rs_send.at[senders], rs_recv.at[senders], rs_s), (x_send.at[senders], x_recv.at[senders], dx_s),
        (y_send.at[senders], y_recv.at[senders], ret_s),
    ]:
        remote(src, dst, sem.at[0], mix_r.at[0], exp_peer(1)).wait_send()

    everything = pl.ds(0, slab + fresh)
    cached = pl.ds(0, slab)

    def sent(at, sem):
        remote(raw.at[0, at], raw.at[0, at], kv_send.at[sem], kv_recv.at[0, 0], ctx_peer(1)).wait_send()

    @pl.when(ci < last)
    def _():
        sent(everything, 0)

    @pl.when(ci > 0)
    def _():
        sent(cached, 1)

    @pl.when(edge)
    def _():
        query_copy(beside_edge).wait_send()

    @pl.when(inner)
    def _():
        @pl.when(ci < across)
        def _():
            sent(everything, 2)

        @pl.when(ci > across)
        def _():
            sent(cached, 2)

        for c in part_copies(near_edge):
            c.wait_send()


def fused_device(
    ctx_count, exp_count, queries, pages, cached_lengths, residual_in, out_weight, norm_gain,
    expert_ids, route_scores, expert_input, expert_output,
):
    fresh, query_width = queries.shape[1:]
    page_size = pages.shape[1]
    slab = page_size - fresh
    rows, width = residual_in.shape[1:]
    top = expert_ids.shape[2]
    hidden_width = expert_input.shape[3]
    experts = ctx_count * exp_count
    capacity = max(2, -(-rows * top // experts))
    stacked = query_width // HEAD * fresh
    vm = pl.BlockSpec(memory_space=pltpu.VMEM)
    hbm = pl.BlockSpec(memory_space=pl.ANY)
    dma = pltpu.SemaphoreType.DMA
    V = pltpu.VMEM
    lanes = exp_count * capacity
    pieces = 4
    halves = 2 if slab % 32 == 0 else 1
    blocks = stacked // HEAD
    context, layer_out = pl.pallas_call(
        functools.partial(fused_kernel, ctx_count, exp_count, capacity),
        out_shape=(V((fresh, query_width), BF), V((rows, width), BF)),
        in_specs=[hbm] * 10,
        out_specs=(vm, vm),
        scratch_shapes=[
            V((1, ctx_count), jnp.int32),
            V((2, fresh, query_width), BF),
            V((rows, width), BF),
            V((1, width), F32),
            V((top, rows), jnp.int32),
            V((top, rows), F32),
            V((ctx_count,) + pages.shape[1:], BF),
            V((ctx_count, slab, 3 * HEAD), BF),
            V((ctx_count * fresh, 3 * HEAD), BF),
            V((2, stacked, HEAD), BF),
            V((2, stacked, HEAD), F32),
            V((2, stacked, 2 * HEAD), F32),
            V((stacked, HEAD), BF),
            V((stacked, HEAD), BF),
            V((blocks, HEAD), F32),
            V((blocks, HEAD), F32),
            V(out_weight.shape, BF),
            V(expert_input.shape[1:], BF),
            V((width, hidden_width), BF),
            V((width, hidden_width), BF),
            V(expert_output.shape[1:], BF),
            V((ctx_count, top, rows), jnp.int32),
            V((ctx_count, top, rows), F32),
            V((ctx_count, top, rows), F32),
            V((ctx_count, lanes, rows), F32),
            V((ctx_count, lanes, rows), F32),
            V((pieces, fresh, width // pieces), F32),
            V((exp_count, pieces, rows, width // pieces), BF),
            V((exp_count, pieces, rows, width // pieces), BF),
            V((rows, width), BF),
            V((ctx_count, rows, width), BF),
            V((exp_count, ctx_count, capacity, width), BF),
            V((exp_count, ctx_count, capacity, width), BF),
            V((exp_count, ctx_count, capacity, width), BF),
            V((exp_count, ctx_count, capacity, width), BF),
            V((ctx_count, rows, width), BF),
            V((ctx_count, rows, width), BF),
            dma((1,)), dma((6,)), dma((3,)), dma((ctx_count, halves + 1)), dma((3,)), dma((2,)), dma((4,)),
            dma((1,)), dma((1,)), dma((1,)), dma((1,)), dma((1,)), dma((pieces,)), dma((1,)), dma((ctx_count,)),
            dma((1,)), dma((ctx_count,)), dma((1,)), dma((ctx_count,)), dma((1,)), dma((ctx_count,)),
        ],
        compiler_params=pltpu.CompilerParams(
            collective_id=0, has_side_effects=True, vmem_limit_bytes=VMEM_LIMIT
        ),
    )(
        cached_lengths, queries[0], pages[0], residual_in[0], norm_gain.reshape(1, width),
        expert_ids[0].T, route_scores[0].T, out_weight, expert_input[0], expert_output[0],
    )
    return context[None], layer_out[None]


def fused_fits(mesh):
    return mesh.shape["rep"] == 1 and mesh.shape["ctx"] == 4


def solution(mesh):
    in_specs = (
        P("groups", "ctx", ("exp", "rep")),
        P("groups", "ctx", None, "exp"),
        P("groups", None),
        P("groups", ("ctx", "exp"), None),
        P(("exp", "rep"), None),
        P(),
        P("groups", ("ctx", "exp"), None),
        P("groups", ("ctx", "exp"), None),
        P(("ctx", "exp"), None, None, "rep"),
        P(("ctx", "exp"), "rep", None),
    )
    out_specs = (P("groups", "ctx", ("exp", "rep")), P("groups", ("ctx", "exp", "rep"), None))
    body = per_device
    if fused_fits(mesh):
        body = functools.partial(fused_device, mesh.shape["ctx"], mesh.shape["exp"])
    return jax.shard_map(
        body, mesh=mesh, in_specs=in_specs, out_specs=out_specs, check_vma=False
    )
```

```python
import functools

import jax
import jax.numpy as jnp
from jax import lax
from jax.experimental import pallas as pl
from jax.experimental.pallas import tpu as pltpu
from jax.sharding import PartitionSpec as P

HEAD = 128


floor_value = -1e30
norm_epsilon = 1e-06


def normalize(hidden, norm_gain):
    widened = hidden.astype(jnp.float32)
    mean_square = jnp.mean(widened * widened, axis=-1, keepdims=True)
    return (widened * lax.rsqrt(mean_square + norm_epsilon) * norm_gain).astype(jnp.bfloat16)


def attend_piece(query_rows, page_rows, allowed):
    scaling = query_rows.shape[-1] ** (-0.5)
    scores = (
        jnp.einsum(
            "rqhe,rke->rqhk", query_rows, page_rows[:, :, 0], preferred_element_type=jnp.float32
        )
        * scaling
    )
    permitted = allowed[:, :, None, :]
    masked = jnp.where(permitted, scores, floor_value)
    peaks = jnp.max(masked, axis=-1)
    weights = jnp.where(permitted, jnp.exp(masked - peaks[..., None]), 0.0)
    totals = jnp.sum(weights, axis=-1)
    summed = jnp.einsum(
        "rqhk,rke->rqhe",
        weights.astype(jnp.bfloat16),
        page_rows[:, :, 1],
        preferred_element_type=jnp.float32,
    )
    return (peaks, totals, summed)


def merge_partials(earlier, later):
    peaks = jnp.maximum(earlier[0], later[0])
    later_scale = jnp.exp(later[0] - peaks)
    totals = later[1] * later_scale
    summed = later[2] * later_scale[..., None]
    return (peaks, totals, summed)


def rows_mask(row_index, lengths, query_positions, slab_size, fresh_block):
    page_size = slab_size + fresh_block
    page_number = row_index // page_size
    offset = row_index - page_number * page_size
    page_count = lengths.shape[1]
    picker = page_number[None, :] == jnp.arange(page_count, dtype=jnp.int32)[:, None]
    live_length = jnp.sum(jnp.where(picker[None], lengths[:, :, None], 0), axis=1)
    in_cache = (offset < slab_size)[None, :] & (offset[None, :] < live_length)
    fresh_position = page_number * fresh_block + offset - slab_size
    in_fresh = (offset >= slab_size)[None, :] & (
        fresh_position[None, :] <= query_positions[:, None]
    )
    return in_cache[:, None, :] | in_fresh[None, :, :]


def per_device(
    queries,
    pages,
    cached_lengths,
    residual_in,
    out_weight,
    norm_gain,
    expert_ids,
    route_scores,
    expert_input,
    expert_output,
):
    requests, fresh_block, query_width = queries.shape
    local_heads = query_width // HEAD
    core_place = lax.axis_index("rep")
    page_place = lax.axis_index("ctx")
    rep_count = lax.axis_size("rep")
    page_size = pages.shape[1]
    slab_size = page_size - fresh_block
    own_positions = page_place * fresh_block + jnp.arange(fresh_block, dtype=jnp.int32)
    query_rows = queries.reshape(requests, fresh_block, local_heads, HEAD)
    start_state = (
        jnp.full((requests, fresh_block, local_heads), floor_value, jnp.float32),
        jnp.zeros((requests, fresh_block, local_heads), jnp.float32),
        jnp.zeros((requests, fresh_block, local_heads, HEAD), jnp.float32),
    )
    page_piece = lax.all_gather(pages, "ctx", axis=1, tiled=True)
    row_index = jnp.arange(page_piece.shape[1], dtype=jnp.int32)
    allowed = rows_mask(row_index, cached_lengths, own_positions, slab_size, fresh_block)
    peaks, totals, summed = merge_partials(
        start_state, attend_piece(query_rows, page_piece, allowed)
    )
    context = (
        (summed / totals[..., None])
        .astype(jnp.bfloat16)
        .reshape(requests, fresh_block, query_width)
    )
    projected = jnp.dot(
        context.reshape(requests * fresh_block, query_width),
        out_weight,
        preferred_element_type=jnp.float32,
    ).reshape(requests, fresh_block, -1)
    token_block = residual_in.shape[1]
    share_size = token_block // rep_count
    own_share = lax.psum_scatter(
        projected.astype(jnp.bfloat16), ("exp", "rep"), scatter_dimension=1, tiled=True
    ).astype(jnp.float32)
    own_residual = lax.dynamic_slice_in_dim(residual_in, core_place * share_size, share_size, 1)
    own_hidden = (own_residual.astype(jnp.float32) + own_share).astype(jnp.bfloat16)
    normed = lax.all_gather(normalize(own_hidden, norm_gain), "rep", axis=1, tiled=True)
    top_count = expert_ids.shape[2]
    expert_count = lax.axis_size("ctx") * lax.axis_size("exp")
    most_rows = max(2, (token_block * top_count + expert_count - 1) // expert_count)
    capacity = requests * most_rows
    model_width = normed.shape[2]
    token_count = requests * token_block
    flat_ids = expert_ids.reshape(-1)
    row_count = flat_ids.shape[0]
    chosen = (flat_ids[:, None] == jnp.arange(expert_count, dtype=jnp.int32)[None, :]).astype(
        jnp.int32
    )
    earlier_rows = jnp.cumsum(chosen, axis=0) - chosen
    slot_rank = jnp.sum(earlier_rows * chosen, axis=1)
    slot_index = flat_ids * capacity + slot_rank
    slot_onehot = (
        slot_index[:, None] == jnp.arange(expert_count * capacity, dtype=jnp.int32)[None, :]
    ).astype(jnp.bfloat16)
    token_onehot = (
        (jnp.arange(row_count, dtype=jnp.int32) // top_count)[:, None]
        == jnp.arange(token_count, dtype=jnp.int32)[None, :]
    ).astype(jnp.bfloat16)
    placement = jnp.dot(slot_onehot.T, token_onehot, preferred_element_type=jnp.float32).astype(
        jnp.bfloat16
    )
    outgoing = jnp.dot(
        placement, normed.reshape(token_count, model_width), preferred_element_type=jnp.float32
    )
    outgoing = outgoing.astype(jnp.bfloat16).reshape(expert_count, capacity, model_width)
    scores_sum = jnp.sum(route_scores, axis=2, keepdims=True)
    combine = (route_scores / scores_sum).astype(jnp.bfloat16).reshape(-1)
    gathering = jnp.dot(
        (token_onehot * combine[:, None]).T, slot_onehot, preferred_element_type=jnp.float32
    ).astype(jnp.bfloat16)
    gate_up = expert_input[0]
    down_weight = expert_output[0]
    arrived_rows = lax.all_to_all(outgoing, ("ctx", "exp"), split_axis=0, concat_axis=0, tiled=True)
    inner_rows = jnp.einsum(
        "nd,dgh->ngh",
        arrived_rows.reshape(-1, model_width),
        gate_up,
        preferred_element_type=jnp.float32,
    )
    activated = (jax.nn.silu(inner_rows[:, 0]) * inner_rows[:, 1]).astype(jnp.bfloat16)
    result = jnp.dot(activated, down_weight, preferred_element_type=jnp.float32).astype(
        jnp.bfloat16
    )
    returned = lax.all_to_all(
        result.reshape(arrived_rows.shape), ("ctx", "exp"), split_axis=0, concat_axis=0, tiled=True
    )
    mixture = jnp.dot(
        gathering,
        returned.reshape(expert_count * capacity, model_width),
        preferred_element_type=jnp.float32,
    )
    own_mixture = lax.psum_scatter(
        mixture.reshape(requests, token_block, model_width).astype(jnp.bfloat16),
        "rep",
        scatter_dimension=1,
        tiled=True,
    ).astype(jnp.float32)
    layer_out = (own_hidden.astype(jnp.float32) + own_mixture).astype(jnp.bfloat16)
    return (context, layer_out)


BF = jnp.bfloat16
F32 = jnp.float32
MESH = pl.DeviceIdType.MESH
VMEM_LIMIT = 60 * 1024 * 1024


def fused_kernel(
    ctx_count, exp_count, capacity,
    lengths, query, page, residual_in, gain_in, ids_in, scores_in, w_out, w_in, w_down,
    context_out, layer_out,
    lens, q_in, residual, gain, ids, scores,
    raw, kv, kv_fresh, q_rows, peak, accum, part_send, part_recv, level_send, level_recv,
    wo, wi, wg, wu, wd,
    ids_all, scores_all, combine_all, place, gather,
    rs_full, rs_send, rs_recv, hidden, nz, x_send, x_recv, y_send, y_recv, mix_send, mix_recv,
    own_sem, in_sem, kv_send, kv_recv, w_sem, q_sem, part_sem, entered,
    ids_s, ids_r, sc_s, sc_r, rs_s, rs_r, nz_s, nz_r, dx_s, dx_r, ret_s, ret_r, mix_s, mix_r,
):
    ci = lax.axis_index("ctx")
    ei = lax.axis_index("exp")
    fresh = q_in.shape[1]
    heads = q_in.shape[2] // HEAD
    slab = kv.shape[1]
    halves = 2 if slab % 32 == 0 else 1
    half_rows = slab // halves
    rows = residual.shape[0]
    width = residual.shape[1]
    top = ids.shape[0]
    stacked = q_rows.shape[1]
    scaling = HEAD ** (-0.5) * 1.4426950408889634

    last = ctx_count - 1
    edge = (ci == 0) | (ci == last)
    inner = (ci > 0) & (ci < last)
    near_edge = jnp.where(ci < 2, 0, last)
    across = last - ci
    far_edge = last - near_edge
    beside_edge = jnp.where(ci == 0, 1, last - 1)

    def ctx_peer(k):
        return {"ctx": lax.rem(ci + k, ctx_count)}

    def exp_peer(k):
        return {"exp": lax.rem(ei + k, exp_count)}

    def remote(src, dst, ss, rs, where):
        return pltpu.make_async_remote_copy(
            src_ref=src, dst_ref=dst, send_sem=ss, recv_sem=rs, device_id=where, device_id_type=MESH
        )

    barrier = pltpu.get_barrier_semaphore()

    @pl.when(inner)
    def _():
        for where in (across, near_edge):
            pl.semaphore_signal(barrier, inc=1, device_id={"ctx": where}, device_id_type=MESH)

    for k in range(1, exp_count):
        pl.semaphore_signal(barrier, inc=1, device_id=exp_peer(k), device_id_type=MESH)

    def tell(n, where):
        pl.semaphore_signal(entered.at[n], inc=1, device_id={"ctx": where}, device_id_type=MESH)

    own_page = pltpu.make_async_copy(page, raw.at[ci], own_sem.at[0])
    own_page.start()
    inputs = [
        pltpu.make_async_copy(src, dst, in_sem.at[n])
        for n, (src, dst) in enumerate(
            [(lengths, lens), (query, q_in.at[0]), (residual_in, residual), (gain_in, gain), (ids_in, ids), (scores_in, scores)]
        )
    ]
    for c in inputs:
        c.start()
    copies_w = [
        pltpu.make_async_copy(w_out, wo, w_sem.at[0]),
        pltpu.make_async_copy(w_in, wi, w_sem.at[1]),
        pltpu.make_async_copy(w_down, wd, w_sem.at[2]),
    ]
    for n in (1, 0, 2):
        copies_w[n].start()

    kv[:, :, 2 * HEAD:] = jnp.ones(kv.shape[:2] + (HEAD,), BF)
    kv_fresh[:, :2 * HEAD] = jnp.zeros((kv_fresh.shape[0], 2 * HEAD), BF)
    kv_fresh[:, 2 * HEAD:] = jnp.ones((kv_fresh.shape[0], HEAD), BF)
    accum[...] = jnp.zeros_like(accum)
    peak[...] = jnp.full_like(peak, floor_value)
    pl.semaphore_wait(barrier, exp_count)

    def send_small(where):
        remote(ids_in, ids_all.at[ci], ids_s.at[0], ids_r.at[0], {"ctx": where}).start()
        remote(scores_in, scores_all.at[ci], sc_s.at[0], sc_r.at[0], {"ctx": where}).start()

    def rows_of(c):
        return pl.ds(c * half_rows, half_rows) if c < halves else pl.ds(slab, fresh)

    def piece(p, c, src, sem, step):
        return remote(src.at[rows_of(c)], raw.at[p, rows_of(c)], kv_send.at[sem], kv_recv.at[p, c], {"ctx": ci + step})

    order_right = [halves] + list(range(halves))
    order_left = list(range(halves))

    def send_right():
        for c in order_right:
            piece(ci, c, page, 0, 1).start()

    def send_left():
        for c in order_left:
            piece(ci, c, page, 1, -1).start()

    def query_copy(where):
        return remote(query, q_in.at[1], q_sem.at[0], q_sem.at[1], {"ctx": where})

    @pl.when(edge)
    def _():
        tell(0, beside_edge)
        send_small(beside_edge)

        @pl.when(ci == 0)
        def _():
            send_right()

        @pl.when(ci > 0)
        def _():
            send_left()

        query_copy(beside_edge).start()

    @pl.when(inner)
    def _():
        send_small(across)

        @pl.when(ci < across)
        def _():
            send_right()

        @pl.when(ci > across)
        def _():
            send_left()

        pl.semaphore_wait(entered.at[0], 1)
        tell(1, across)
        send_small(near_edge)

        @pl.when(ci < across)
        def _():
            send_left()

        @pl.when(ci > across)
        def _():
            send_right()

    def stage_queries(n):
        for h in range(heads):
            q_rows[n, h * fresh:(h + 1) * fresh, :] = q_in[n, :, h * HEAD:(h + 1) * HEAD]

    inputs[0].wait()
    inputs[1].wait()
    stage_queries(0)

    step = next(n for n in (4, 2, 1) if heads % n == 0)
    page_number = lax.broadcasted_iota(jnp.int32, (1, ctx_count), 1)
    slab_row = lax.broadcasted_iota(jnp.int32, (1, slab), 1).astype(F32)

    def split(p, c):
        both = pltpu.einshape("sgh->gsh", raw[p, rows_of(c)])
        if c < halves:
            kv[p, rows_of(c), :HEAD] = both[0]
            kv[p, rows_of(c), HEAD:2 * HEAD] = both[1]
        else:
            at = pl.ds(pl.multiple_of(p * fresh, fresh), fresh)
            kv_fresh[at, :HEAD] = both[0]
            kv_fresh[at, HEAD:2 * HEAD] = both[1]

    def attend(n, source, bias, after=None):
        keys = source[:, :HEAD]
        values = source[:, HEAD:]
        count = keys.shape[0]
        for h in range(0, heads, step):
            sl = slice(h * fresh, (h + step) * fresh)
            s = lax.dot_general(
                q_rows[n, sl, :], keys, (((1,), (1,)), ((), ())), preferred_element_type=F32
            )
            s = (s.reshape(step, fresh, count) + bias[None]).reshape(step * fresh, count)
            old = peak[n, sl, :]
            now = jnp.maximum(old, jnp.max(s, axis=1, keepdims=True))
            w = jnp.exp2((s - now[:, :1]) * scaling)
            fade = jnp.exp2((old - now) * scaling)
            accum[n, sl, :] = accum[n, sl, :] * jnp.concatenate([fade, fade], 1) + jnp.dot(
                w.astype(BF), values, preferred_element_type=F32
            )
            peak[n, sl, :] = now
            if after:
                after(sl)

    def attend_page(n, p, after=None):
        live = jnp.sum(jnp.where(page_number == p, lens[...], 0).astype(F32), axis=1, keepdims=True)
        attend(n, kv.at[p], jnp.where(slab_row < live, 0.0, floor_value), after)

    def attend_fresh(n, home, first, count):
        count *= fresh
        at = pl.ds(pl.multiple_of(first * fresh, fresh), count)
        row = lax.broadcasted_iota(jnp.int32, (fresh, count), 1) + first * fresh
        position = lax.broadcasted_iota(jnp.int32, (fresh, count), 0) + home * fresh
        attend(n, kv_fresh.at[at], jnp.where(row <= position, 0.0, floor_value))

    own_page.wait()
    for c in order_right:
        split(ci, c)
    attend_page(0, ci)

    depth = next(n for n in (256, 128, 64, 32, 16) if width % n == 0)
    copies_w[1].wait()

    def unpack(i, carry):
        at = pl.ds(pl.multiple_of(i * depth, depth), depth)
        block = pltpu.einshape("dgh->gdh", wi[at])
        wg[at, :] = block[0]
        wu[at, :] = block[1]
        return carry

    lax.fori_loop(0, width // depth, unpack, 0)

    @pl.when(inner)
    def _():
        pl.semaphore_wait(entered.at[1], 1)
        tell(2, near_edge)
        send_small(far_edge)

    @pl.when(edge)
    def _():
        pl.semaphore_wait(entered.at[2], 1)
        send_small(last - beside_edge)
        send_small(far_edge)

    for c in inputs[2:]:
        c.wait()
    ids_all[ci] = ids[...]
    scores_all[ci] = scores[...]

    def route():
        others = pl.ds(0, last)
        remote(ids_all.at[others], ids_all.at[others], ids_s.at[0], ids_r.at[0], ctx_peer(1)).wait_recv()
        remote(scores_all.at[others], scores_all.at[others], sc_s.at[0], sc_r.at[0], ctx_peer(1)).wait_recv()
        lanes = exp_count * capacity
        lane = lax.broadcasted_iota(jnp.int32, (lanes, rows), 0)
        wanted = ci * exp_count + lax.rem(ei + lane // capacity, exp_count)
        seat = (lane - lane // capacity * capacity).astype(F32)
        earlier = (
            lax.broadcasted_iota(jnp.int32, (rows, rows), 0)
            < lax.broadcasted_iota(jnp.int32, (rows, rows), 1)
        ).astype(F32)
        for k in range(ctx_count):
            given = scores_all[k]
            combine_all[k] = (given / jnp.sum(given, axis=0, keepdims=True)).astype(BF).astype(F32)
        for k in range(ctx_count):
            chosen = jnp.zeros((lanes, rows), F32)
            portion = jnp.zeros((lanes, rows), F32)
            for j in range(top):
                hit = ids_all[k, j:j + 1, :] == wanted
                chosen = jnp.where(hit, 1.0, chosen)
                portion = jnp.where(hit, combine_all[k, j:j + 1, :], portion)
            rank = jnp.dot(chosen.astype(BF), earlier.astype(BF), preferred_element_type=F32)
            seated = (chosen > 0.5) & (rank == seat)
            place[k] = jnp.where(seated, 1.0, 0.0)
            gather[k] = jnp.where(seated, portion, 0.0)

    def arrive(p, c):
        piece(p, c, raw.at[p], 0, 1).wait_recv()

    def pass_on(c):
        @pl.when(ci < across)
        def _():
            piece(near_edge, c, raw.at[near_edge], 2, 1).start()

        if c < halves:
            @pl.when(ci > across)
            def _():
                piece(near_edge, c, raw.at[near_edge], 2, -1).start()

    def arrive_fresh(p):
        arrive(p, halves)
        split(p, halves)

    block_rows = stacked // level_send.shape[0]

    def part_copy(sl, where):
        return remote(part_send.at[sl], part_recv.at[sl], part_sem.at[0], part_sem.at[1], {"ctx": where})

    def level_copy(where):
        return remote(level_send, level_recv, part_sem.at[2], part_sem.at[3], {"ctx": where})

    @pl.when(inner)
    def _():
        @pl.when(ci < across)
        def _():
            arrive(near_edge, halves)
            pass_on(halves)
            split(near_edge, halves)

        @pl.when(ci > across)
        def _():
            arrive_fresh(across)

        for c in range(halves):
            arrive(near_edge, c)
            pass_on(c)
            split(near_edge, c)
            arrive(across, c)
            split(across, c)
        attend_page(0, near_edge)
        attend_page(0, across)
        query_copy(ci).wait_recv()
        stage_queries(1)
        attend_page(1, across)

        @pl.when(ci > across)
        def _():
            arrive_fresh(far_edge)
            attend_fresh(1, near_edge, 0, ctx_count // 2)

        attend_fresh(0, ci, 0, ctx_count)
        route()
        for c in range(halves):
            arrive(far_edge, c)
            split(far_edge, c)

        def finish(sl):
            for b in range(sl.start // block_rows, sl.stop // block_rows):
                at = slice(b * block_rows, (b + 1) * block_rows)
                whole = accum[1, at, HEAD:]
                part_send[at, :] = (accum[1, at, :HEAD] / whole).astype(BF)
                level = peak[1, at, :] * scaling + jnp.log(whole) * 1.4426950408889634
                level_send[b:b + 1, :] = jnp.transpose(level)[:1, :]
            part_copy(sl, near_edge).start()

        attend_page(1, far_edge, finish)
        level_copy(near_edge).start()
        attend_page(0, far_edge)
        for h in range(heads):
            sl = slice(h * fresh, (h + 1) * fresh)
            context_out[:, h * HEAD:(h + 1) * HEAD] = (accum[0, sl, :HEAD] / accum[0, sl, HEAD:]).astype(BF)

    @pl.when(edge)
    def _():
        @pl.when(ci > 0)
        def _():
            arrive_fresh(beside_edge)

        attend_fresh(0, ci, jnp.where(ci == 0, 0, ctx_count // 2), ctx_count // 2)
        for c in range(halves):
            arrive(beside_edge, c)
            split(beside_edge, c)
        attend_page(0, beside_edge)
        route()
        part_copy(slice(0, stacked), ci).wait_recv()
        level_copy(ci).wait_recv()
        per = block_rows // fresh
        for b in range(stacked // block_rows):
            sl = slice(b * block_rows, (b + 1) * block_rows)
            theirs = jnp.transpose(jnp.broadcast_to(level_recv[b:b + 1, :], (HEAD, block_rows)))
            ours = peak[0, sl, :] * scaling
            level = jnp.maximum(ours, theirs)
            fade = jnp.exp2(ours - level)
            share = jnp.exp2(theirs - level)
            merged = (accum[0, sl, :HEAD] * fade + part_recv[sl, :].astype(F32) * share) / (
                accum[0, sl, HEAD:] * fade + share
            )
            for h in range(per):
                at = b * per + h
                context_out[:, at * HEAD:(at + 1) * HEAD] = merged[h * fresh:(h + 1) * fresh, :].astype(BF)

    copies_w[0].wait()

    pieces = 4
    piece_width = width // pieces
    senders = pl.ds(1, exp_count - 1)
    for n in range(pieces):
        cols = slice(n * piece_width, (n + 1) * piece_width)
        part = jnp.dot(context_out[...], wo[:, cols], preferred_element_type=F32)
        rs_full[n] = part
        for k in range(1, exp_count):
            at = pl.ds(pl.multiple_of(lax.rem(ei + k, exp_count) * rows, rows), rows)
            rs_send[k, n] = rs_full[n, at, :].astype(BF)
            remote(rs_send.at[k, n], rs_recv.at[k, n], rs_s.at[0], rs_r.at[n], exp_peer(k)).start()
    mine = pl.ds(pl.multiple_of(ei * rows, rows), rows)
    square = jnp.zeros((rows, 1), F32)
    for n in range(pieces):
        cols = slice(n * piece_width, (n + 1) * piece_width)
        share = rs_full[n, mine, :]
        remote(rs_send.at[senders, n], rs_recv.at[senders, n], rs_s.at[0], rs_r.at[n], exp_peer(1)).wait_recv()
        for k in range(1, exp_count):
            share = share + rs_recv[k, n].astype(F32)
        h = (residual[:, cols].astype(F32) + share).astype(BF)
        hidden[:, cols] = h
        wide = h.astype(F32)
        square = square + jnp.sum(wide * wide, axis=1, keepdims=True)
    inverse = lax.rsqrt(square / width + norm_epsilon)
    nz[ci] = (hidden[...].astype(F32) * inverse * gain[...]).astype(BF)

    middle = last / 2
    send_table, work_table = [], []
    for c in range(ctx_count):
        others = [p for p in range(ctx_count) if p != c]
        send_table.append(sorted(others, key=lambda p: (abs(p - c) % last, abs(p - middle))))
        work_table.append([c] + sorted(others, key=lambda p: ((abs(p - c) - 1) % (last - 1) if last > 1 else 0, abs(p - middle))))

    def lookup(table, n):
        value = jnp.int32(table[0][n])
        for c in range(1, ctx_count):
            value = jnp.where(ci == c, table[c][n], value)
        return value

    def nz_copy(p, where):
        return remote(nz.at[p], nz.at[p], nz_s.at[0], nz_r.at[p], {"ctx": where})

    for n in range(last):
        nz_copy(ci, lookup(send_table, n)).start()

    places = [lookup(work_table, n) for n in range(ctx_count)]

    def dx_copy(j, n):
        p = places[n]
        return remote(x_send.at[j, p], x_recv.at[j, p], dx_s.at[0], dx_r.at[p], exp_peer(1 if j is senders else j))

    def ret_copy(j, n):
        p = places[n]
        return remote(y_send.at[j, p], y_recv.at[j, p], ret_s.at[0], ret_r.at[p], exp_peer(1 if j is senders else exp_count - j))

    def mix_copy(n):
        p = places[n]
        return remote(mix_send.at[p], mix_recv.at[ci], mix_s.at[0], mix_r.at[ci], {"ctx": p})

    def dispatch(n):
        p = places[n]
        if n:
            nz_copy(p, p).wait_recv()
        routed = jnp.dot(place[p].astype(BF), nz[p], preferred_element_type=F32)
        for j in list(range(1, exp_count)) + [0]:
            block = routed[j * capacity:(j + 1) * capacity].astype(BF)
            if j == 0:
                x_recv[0, p] = block
            else:
                x_send[j, p] = block
                dx_copy(j, n).start()

    def experts(n):
        p = places[n]
        dx_copy(senders, n).wait_recv()
        x = jnp.concatenate([x_recv[j, p].astype(F32) for j in range(exp_count)], 0).astype(BF)
        gate = jnp.dot(x, wg[...], preferred_element_type=F32)
        up = jnp.dot(x, wu[...], preferred_element_type=F32)
        act = (gate / (1.0 + jnp.exp(-gate)) * up).astype(BF)
        result = jnp.dot(act, wd[...], preferred_element_type=F32)
        for j in list(range(1, exp_count)) + [0]:
            block = result[j * capacity:(j + 1) * capacity].astype(BF)
            if j == 0:
                y_recv[0, p] = block
            else:
                y_send[j, p] = block
                ret_copy(j, n).start()

    def mixing(n):
        p = places[n]
        ret_copy(senders, n).wait_recv()
        rows_p = jnp.concatenate([y_recv[j, p].astype(F32) for j in range(exp_count)], 0).astype(BF)
        mixed = lax.dot_general(
            gather[p].astype(BF), rows_p, (((0,), (0,)), ((), ())), preferred_element_type=F32
        )
        if n == 0:
            return mixed
        mix_send[p] = mixed.astype(BF)
        mix_copy(n).start()

    dispatch(0)
    for n in range(1, ctx_count):
        if n == 2:
            pl.when(inner)(lambda: experts(1))
        dispatch(n)
        if n == 1:
            copies_w[2].wait()
        if n == 2:
            pl.when(edge)(lambda: experts(1))
        else:
            experts(n - 1)
        if n > 2:
            mixing(n - 2)
    experts(ctx_count - 1)
    for n in range(max(1, ctx_count - 2), ctx_count):
        mixing(n)
    out = hidden[...].astype(F32) + mixing(0)
    for n in range(1, ctx_count):
        p = places[n]
        remote(mix_send.at[p], mix_recv.at[p], mix_s.at[0], mix_r.at[p], {"ctx": p}).wait_recv()
        out = out + mix_recv[p].astype(F32)
    layer_out[...] = out.astype(BF)

    others = pl.ds(0, last)
    for src, dst, sem in [
        (ids_all.at[others], ids_all.at[others], ids_s), (scores_all.at[others], scores_all.at[others], sc_s),
        (nz.at[others], nz.at[others], nz_s), (mix_send.at[others], mix_recv.at[others], mix_s),
    ]:
        remote(src, dst, sem.at[0], mix_r.at[0], ctx_peer(1)).wait_send()
    for src, dst, sem in [
        (rs_send.at[senders], rs_recv.at[senders], rs_s), (x_send.at[senders], x_recv.at[senders], dx_s),
        (y_send.at[senders], y_recv.at[senders], ret_s),
    ]:
        remote(src, dst, sem.at[0], mix_r.at[0], exp_peer(1)).wait_send()

    everything = pl.ds(0, slab + fresh)
    cached = pl.ds(0, slab)

    def sent(at, sem):
        remote(raw.at[0, at], raw.at[0, at], kv_send.at[sem], kv_recv.at[0, 0], ctx_peer(1)).wait_send()

    @pl.when(ci < last)
    def _():
        sent(everything, 0)

    @pl.when(ci > 0)
    def _():
        sent(cached, 1)

    @pl.when(edge)
    def _():
        query_copy(beside_edge).wait_send()

    @pl.when(inner)
    def _():
        @pl.when(ci < across)
        def _():
            sent(everything, 2)

        @pl.when(ci > across)
        def _():
            sent(cached, 2)

        part_copy(slice(0, stacked), near_edge).wait_send()
        level_copy(near_edge).wait_send()


def settle(context, layer, context_out, layer_out, sem):
    copies = [
        pltpu.make_async_copy(context, context_out, sem.at[0]),
        pltpu.make_async_copy(layer, layer_out, sem.at[1]),
    ]
    for c in copies:
        c.start()
    for c in copies:
        c.wait()


def fused_device(
    ctx_count, exp_count, queries, pages, cached_lengths, residual_in, out_weight, norm_gain,
    expert_ids, route_scores, expert_input, expert_output,
):
    fresh, query_width = queries.shape[1:]
    page_size = pages.shape[1]
    slab = page_size - fresh
    rows, width = residual_in.shape[1:]
    top = expert_ids.shape[2]
    hidden_width = expert_input.shape[3]
    experts = ctx_count * exp_count
    capacity = max(2, -(-rows * top // experts))
    stacked = query_width // HEAD * fresh
    vm = pl.BlockSpec(memory_space=pltpu.VMEM)
    hbm = pl.BlockSpec(memory_space=pl.ANY)
    dma = pltpu.SemaphoreType.DMA
    V = pltpu.VMEM
    lanes = exp_count * capacity
    pieces = 4
    halves = 2 if slab % 32 == 0 else 1
    blocks = stacked // HEAD
    context, layer_out = pl.pallas_call(
        functools.partial(fused_kernel, ctx_count, exp_count, capacity),
        out_shape=(V((fresh, query_width), BF), V((rows, width), BF)),
        in_specs=[hbm] * 10,
        out_specs=(vm, vm),
        scratch_shapes=[
            V((1, ctx_count), jnp.int32),
            V((2, fresh, query_width), BF),
            V((rows, width), BF),
            V((1, width), F32),
            V((top, rows), jnp.int32),
            V((top, rows), F32),
            V((ctx_count,) + pages.shape[1:], BF),
            V((ctx_count, slab, 3 * HEAD), BF),
            V((ctx_count * fresh, 3 * HEAD), BF),
            V((2, stacked, HEAD), BF),
            V((2, stacked, HEAD), F32),
            V((2, stacked, 2 * HEAD), F32),
            V((stacked, HEAD), BF),
            V((stacked, HEAD), BF),
            V((blocks, HEAD), F32),
            V((blocks, HEAD), F32),
            V(out_weight.shape, BF),
            V(expert_input.shape[1:], BF),
            V((width, hidden_width), BF),
            V((width, hidden_width), BF),
            V(expert_output.shape[1:], BF),
            V((ctx_count, top, rows), jnp.int32),
            V((ctx_count, top, rows), F32),
            V((ctx_count, top, rows), F32),
            V((ctx_count, lanes, rows), F32),
            V((ctx_count, lanes, rows), F32),
            V((pieces, fresh, width // pieces), F32),
            V((exp_count, pieces, rows, width // pieces), BF),
            V((exp_count, pieces, rows, width // pieces), BF),
            V((rows, width), BF),
            V((ctx_count, rows, width), BF),
            V((exp_count, ctx_count, capacity, width), BF),
            V((exp_count, ctx_count, capacity, width), BF),
            V((exp_count, ctx_count, capacity, width), BF),
            V((exp_count, ctx_count, capacity, width), BF),
            V((ctx_count, rows, width), BF),
            V((ctx_count, rows, width), BF),
            dma((1,)), dma((6,)), dma((3,)), dma((ctx_count, halves + 1)), dma((3,)), dma((2,)), dma((4,)),
            pltpu.SemaphoreType.REGULAR((3,)),
            dma((1,)), dma((1,)), dma((1,)), dma((1,)), dma((1,)), dma((pieces,)), dma((1,)), dma((ctx_count,)),
            dma((1,)), dma((ctx_count,)), dma((1,)), dma((ctx_count,)), dma((1,)), dma((ctx_count,)),
        ],
        compiler_params=pltpu.CompilerParams(
            collective_id=0, has_side_effects=True, vmem_limit_bytes=VMEM_LIMIT
        ),
    )(
        cached_lengths, queries[0], pages[0], residual_in[0], norm_gain.reshape(1, width),
        expert_ids[0].T, route_scores[0].T, out_weight, expert_input[0], expert_output[0],
    )
    context, layer_out = pl.pallas_call(
        settle,
        out_shape=(
            jax.ShapeDtypeStruct(context.shape, BF),
            jax.ShapeDtypeStruct(layer_out.shape, BF),
        ),
        in_specs=[vm, vm],
        out_specs=(hbm, hbm),
        scratch_shapes=[dma((2,))],
    )(
        pltpu.with_memory_space_constraint(context, pltpu.VMEM),
        pltpu.with_memory_space_constraint(layer_out, pltpu.VMEM),
    )
    return context[None], layer_out[None]


def fused_fits(mesh):
    return mesh.shape["rep"] == 1 and mesh.shape["ctx"] == 4


def solution(mesh):
    in_specs = (
        P("groups", "ctx", ("exp", "rep")),
        P("groups", "ctx", None, "exp"),
        P("groups", None),
        P("groups", ("ctx", "exp"), None),
        P(("exp", "rep"), None),
        P(),
        P("groups", ("ctx", "exp"), None),
        P("groups", ("ctx", "exp"), None),
        P(("ctx", "exp"), None, None, "rep"),
        P(("ctx", "exp"), "rep", None),
    )
    out_specs = (P("groups", "ctx", ("exp", "rep")), P("groups", ("ctx", "exp", "rep"), None))
    body = per_device
    if fused_fits(mesh):
        body = functools.partial(fused_device, mesh.shape["ctx"], mesh.shape["exp"])
    return jax.shard_map(
        body, mesh=mesh, in_specs=in_specs, out_specs=out_specs, check_vma=False
    )
```

```python
import functools

import jax
import jax.numpy as jnp
from jax import lax
from jax.experimental import pallas as pl
from jax.experimental.pallas import tpu as pltpu
from jax.sharding import PartitionSpec as P

HEAD = 128


floor_value = -1e30
norm_epsilon = 1e-06


def normalize(hidden, norm_gain):
    widened = hidden.astype(jnp.float32)
    mean_square = jnp.mean(widened * widened, axis=-1, keepdims=True)
    return (widened * lax.rsqrt(mean_square + norm_epsilon) * norm_gain).astype(jnp.bfloat16)


def attend_piece(query_rows, page_rows, allowed):
    scaling = query_rows.shape[-1] ** (-0.5)
    scores = (
        jnp.einsum(
            "rqhe,rke->rqhk", query_rows, page_rows[:, :, 0], preferred_element_type=jnp.float32
        )
        * scaling
    )
    permitted = allowed[:, :, None, :]
    masked = jnp.where(permitted, scores, floor_value)
    peaks = jnp.max(masked, axis=-1)
    weights = jnp.where(permitted, jnp.exp(masked - peaks[..., None]), 0.0)
    totals = jnp.sum(weights, axis=-1)
    summed = jnp.einsum(
        "rqhk,rke->rqhe",
        weights.astype(jnp.bfloat16),
        page_rows[:, :, 1],
        preferred_element_type=jnp.float32,
    )
    return (peaks, totals, summed)


def merge_partials(earlier, later):
    peaks = jnp.maximum(earlier[0], later[0])
    later_scale = jnp.exp(later[0] - peaks)
    totals = later[1] * later_scale
    summed = later[2] * later_scale[..., None]
    return (peaks, totals, summed)


def rows_mask(row_index, lengths, query_positions, slab_size, fresh_block):
    page_size = slab_size + fresh_block
    page_number = row_index // page_size
    offset = row_index - page_number * page_size
    page_count = lengths.shape[1]
    picker = page_number[None, :] == jnp.arange(page_count, dtype=jnp.int32)[:, None]
    live_length = jnp.sum(jnp.where(picker[None], lengths[:, :, None], 0), axis=1)
    in_cache = (offset < slab_size)[None, :] & (offset[None, :] < live_length)
    fresh_position = page_number * fresh_block + offset - slab_size
    in_fresh = (offset >= slab_size)[None, :] & (
        fresh_position[None, :] <= query_positions[:, None]
    )
    return in_cache[:, None, :] | in_fresh[None, :, :]


def per_device(
    queries,
    pages,
    cached_lengths,
    residual_in,
    out_weight,
    norm_gain,
    expert_ids,
    route_scores,
    expert_input,
    expert_output,
):
    requests, fresh_block, query_width = queries.shape
    local_heads = query_width // HEAD
    core_place = lax.axis_index("rep")
    page_place = lax.axis_index("ctx")
    rep_count = lax.axis_size("rep")
    page_size = pages.shape[1]
    slab_size = page_size - fresh_block
    own_positions = page_place * fresh_block + jnp.arange(fresh_block, dtype=jnp.int32)
    query_rows = queries.reshape(requests, fresh_block, local_heads, HEAD)
    start_state = (
        jnp.full((requests, fresh_block, local_heads), floor_value, jnp.float32),
        jnp.zeros((requests, fresh_block, local_heads), jnp.float32),
        jnp.zeros((requests, fresh_block, local_heads, HEAD), jnp.float32),
    )
    page_piece = lax.all_gather(pages, "ctx", axis=1, tiled=True)
    row_index = jnp.arange(page_piece.shape[1], dtype=jnp.int32)
    allowed = rows_mask(row_index, cached_lengths, own_positions, slab_size, fresh_block)
    peaks, totals, summed = merge_partials(
        start_state, attend_piece(query_rows, page_piece, allowed)
    )
    context = (
        (summed / totals[..., None])
        .astype(jnp.bfloat16)
        .reshape(requests, fresh_block, query_width)
    )
    projected = jnp.dot(
        context.reshape(requests * fresh_block, query_width),
        out_weight,
        preferred_element_type=jnp.float32,
    ).reshape(requests, fresh_block, -1)
    token_block = residual_in.shape[1]
    share_size = token_block // rep_count
    own_share = lax.psum_scatter(
        projected.astype(jnp.bfloat16), ("exp", "rep"), scatter_dimension=1, tiled=True
    ).astype(jnp.float32)
    own_residual = lax.dynamic_slice_in_dim(residual_in, core_place * share_size, share_size, 1)
    own_hidden = (own_residual.astype(jnp.float32) + own_share).astype(jnp.bfloat16)
    normed = lax.all_gather(normalize(own_hidden, norm_gain), "rep", axis=1, tiled=True)
    top_count = expert_ids.shape[2]
    expert_count = lax.axis_size("ctx") * lax.axis_size("exp")
    most_rows = max(2, (token_block * top_count + expert_count - 1) // expert_count)
    capacity = requests * most_rows
    model_width = normed.shape[2]
    token_count = requests * token_block
    flat_ids = expert_ids.reshape(-1)
    row_count = flat_ids.shape[0]
    chosen = (flat_ids[:, None] == jnp.arange(expert_count, dtype=jnp.int32)[None, :]).astype(
        jnp.int32
    )
    earlier_rows = jnp.cumsum(chosen, axis=0) - chosen
    slot_rank = jnp.sum(earlier_rows * chosen, axis=1)
    slot_index = flat_ids * capacity + slot_rank
    slot_onehot = (
        slot_index[:, None] == jnp.arange(expert_count * capacity, dtype=jnp.int32)[None, :]
    ).astype(jnp.bfloat16)
    token_onehot = (
        (jnp.arange(row_count, dtype=jnp.int32) // top_count)[:, None]
        == jnp.arange(token_count, dtype=jnp.int32)[None, :]
    ).astype(jnp.bfloat16)
    placement = jnp.dot(slot_onehot.T, token_onehot, preferred_element_type=jnp.float32).astype(
        jnp.bfloat16
    )
    outgoing = jnp.dot(
        placement, normed.reshape(token_count, model_width), preferred_element_type=jnp.float32
    )
    outgoing = outgoing.astype(jnp.bfloat16).reshape(expert_count, capacity, model_width)
    scores_sum = jnp.sum(route_scores, axis=2, keepdims=True)
    combine = (route_scores / scores_sum).astype(jnp.bfloat16).reshape(-1)
    gathering = jnp.dot(
        (token_onehot * combine[:, None]).T, slot_onehot, preferred_element_type=jnp.float32
    ).astype(jnp.bfloat16)
    gate_up = expert_input[0]
    down_weight = expert_output[0]
    arrived_rows = lax.all_to_all(outgoing, ("ctx", "exp"), split_axis=0, concat_axis=0, tiled=True)
    inner_rows = jnp.einsum(
        "nd,dgh->ngh",
        arrived_rows.reshape(-1, model_width),
        gate_up,
        preferred_element_type=jnp.float32,
    )
    activated = (jax.nn.silu(inner_rows[:, 0]) * inner_rows[:, 1]).astype(jnp.bfloat16)
    result = jnp.dot(activated, down_weight, preferred_element_type=jnp.float32).astype(
        jnp.bfloat16
    )
    returned = lax.all_to_all(
        result.reshape(arrived_rows.shape), ("ctx", "exp"), split_axis=0, concat_axis=0, tiled=True
    )
    mixture = jnp.dot(
        gathering,
        returned.reshape(expert_count * capacity, model_width),
        preferred_element_type=jnp.float32,
    )
    own_mixture = lax.psum_scatter(
        mixture.reshape(requests, token_block, model_width).astype(jnp.bfloat16),
        "rep",
        scatter_dimension=1,
        tiled=True,
    ).astype(jnp.float32)
    layer_out = (own_hidden.astype(jnp.float32) + own_mixture).astype(jnp.bfloat16)
    return (context, layer_out)


BF = jnp.bfloat16
F32 = jnp.float32
MESH = pl.DeviceIdType.MESH
VMEM_LIMIT = 60 * 1024 * 1024


def fused_kernel(
    ctx_count, exp_count, capacity,
    lengths, query, page, residual_in, gain_in, ids_in, scores_in, w_out, w_in, w_down,
    context_out, layer_out,
    lens, q_in, residual, gain, ids, scores,
    raw, kv, kv_fresh, q_rows, peak, accum, part_send, part_recv, level_send, level_recv,
    wo, wi, wg, wu, wd,
    ids_all, scores_all, combine_all, place, gather,
    rs_full, rs_send, rs_recv, hidden, nz, x_send, x_recv, y_send, y_recv, mix_send, mix_recv,
    own_sem, in_sem, kv_send, kv_recv, w_sem, q_sem, part_sem, entered,
    ids_s, ids_r, sc_s, sc_r, rs_s, rs_r, nz_s, nz_r, dx_s, dx_r, ret_s, ret_r, mix_s, mix_r,
):
    ci = lax.axis_index("ctx")
    ei = lax.axis_index("exp")
    fresh = q_in.shape[1]
    heads = q_in.shape[2] // HEAD
    slab = kv.shape[1]
    halves = 2 if slab % 32 == 0 else 1
    half_rows = slab // halves
    rows = residual.shape[0]
    width = residual.shape[1]
    top = ids.shape[0]
    stacked = q_rows.shape[1]
    scaling = HEAD ** (-0.5) * 1.4426950408889634

    last = ctx_count - 1
    edge = (ci == 0) | (ci == last)
    inner = (ci > 0) & (ci < last)
    near_edge = jnp.where(ci < 2, 0, last)
    across = last - ci
    far_edge = last - near_edge
    beside_edge = jnp.where(ci == 0, 1, last - 1)

    def ctx_peer(k):
        return {"ctx": lax.rem(ci + k, ctx_count)}

    def exp_peer(k):
        return {"exp": lax.rem(ei + k, exp_count)}

    def remote(src, dst, ss, rs, where):
        return pltpu.make_async_remote_copy(
            src_ref=src, dst_ref=dst, send_sem=ss, recv_sem=rs, device_id=where, device_id_type=MESH
        )

    barrier = pltpu.get_barrier_semaphore()

    @pl.when(inner)
    def _():
        for where in (across, near_edge):
            pl.semaphore_signal(barrier, inc=1, device_id={"ctx": where}, device_id_type=MESH)

    for k in range(1, exp_count):
        pl.semaphore_signal(barrier, inc=1, device_id=exp_peer(k), device_id_type=MESH)

    def tell(n, where):
        pl.semaphore_signal(entered.at[n], inc=1, device_id={"ctx": where}, device_id_type=MESH)

    own_page = pltpu.make_async_copy(page, raw.at[ci], own_sem.at[0])
    own_page.start()
    inputs = [
        pltpu.make_async_copy(src, dst, in_sem.at[n])
        for n, (src, dst) in enumerate(
            [(lengths, lens), (query, q_in.at[0]), (residual_in, residual), (gain_in, gain), (ids_in, ids), (scores_in, scores)]
        )
    ]
    for c in inputs:
        c.start()
    copies_w = [
        pltpu.make_async_copy(w_out, wo, w_sem.at[0]),
        pltpu.make_async_copy(w_in, wi, w_sem.at[1]),
        pltpu.make_async_copy(w_down, wd, w_sem.at[2]),
    ]
    for n in (1, 0, 2):
        copies_w[n].start()

    kv[:, :, 2 * HEAD:] = jnp.ones(kv.shape[:2] + (HEAD,), BF)
    kv_fresh[:, :2 * HEAD] = jnp.zeros((kv_fresh.shape[0], 2 * HEAD), BF)
    kv_fresh[:, 2 * HEAD:] = jnp.ones((kv_fresh.shape[0], HEAD), BF)
    accum[...] = jnp.zeros_like(accum)
    peak[...] = jnp.full_like(peak, floor_value)
    pl.semaphore_wait(barrier, exp_count)

    def send_small(where):
        remote(ids_in, ids_all.at[ci], ids_s.at[0], ids_r.at[0], {"ctx": where}).start()
        remote(scores_in, scores_all.at[ci], sc_s.at[0], sc_r.at[0], {"ctx": where}).start()

    def rows_of(c):
        return pl.ds(c * half_rows, half_rows) if c < halves else pl.ds(slab, fresh)

    def piece(p, c, src, sem, step):
        return remote(src.at[rows_of(c)], raw.at[p, rows_of(c)], kv_send.at[sem], kv_recv.at[p, c], {"ctx": ci + step})

    order_right = [halves] + list(range(halves))
    order_left = list(range(halves))

    def send_right():
        for c in order_right:
            piece(ci, c, page, 0, 1).start()

    def send_left():
        for c in order_left:
            piece(ci, c, page, 1, -1).start()

    def query_copy(where):
        return remote(query, q_in.at[1], q_sem.at[0], q_sem.at[1], {"ctx": where})

    @pl.when(edge)
    def _():
        tell(0, beside_edge)
        send_small(beside_edge)

        @pl.when(ci == 0)
        def _():
            send_right()

        @pl.when(ci > 0)
        def _():
            send_left()

        query_copy(beside_edge).start()

    @pl.when(inner)
    def _():
        send_small(across)

        @pl.when(ci < across)
        def _():
            send_right()

        @pl.when(ci > across)
        def _():
            send_left()

        pl.semaphore_wait(entered.at[0], 1)
        tell(1, across)
        send_small(near_edge)

        @pl.when(ci < across)
        def _():
            send_left()

        @pl.when(ci > across)
        def _():
            send_right()

    def stage_queries(n):
        for h in range(heads):
            q_rows[n, h * fresh:(h + 1) * fresh, :] = q_in[n, :, h * HEAD:(h + 1) * HEAD]

    inputs[0].wait()
    inputs[1].wait()
    stage_queries(0)

    step = next(n for n in (4, 2, 1) if heads % n == 0)
    page_number = lax.broadcasted_iota(jnp.int32, (1, ctx_count), 1)
    slab_row = lax.broadcasted_iota(jnp.int32, (1, slab), 1).astype(F32)

    def split(p, c):
        both = pltpu.einshape("sgh->gsh", raw[p, rows_of(c)])
        if c < halves:
            kv[p, rows_of(c), :HEAD] = both[0]
            kv[p, rows_of(c), HEAD:2 * HEAD] = both[1]
        else:
            at = pl.ds(pl.multiple_of(p * fresh, fresh), fresh)
            kv_fresh[at, :HEAD] = both[0]
            kv_fresh[at, HEAD:2 * HEAD] = both[1]

    def attend(n, source, bias, after=None):
        keys = source[:, :HEAD]
        values = source[:, HEAD:]
        count = keys.shape[0]
        for h in range(0, heads, step):
            sl = slice(h * fresh, (h + step) * fresh)
            s = lax.dot_general(
                q_rows[n, sl, :], keys, (((1,), (1,)), ((), ())), preferred_element_type=F32
            )
            s = (s.reshape(step, fresh, count) + bias[None]).reshape(step * fresh, count)
            old = peak[n, sl, :]
            now = jnp.maximum(old, jnp.max(s, axis=1, keepdims=True))
            w = jnp.exp2((s - now[:, :1]) * scaling)
            fade = jnp.exp2((old - now) * scaling)
            accum[n, sl, :] = accum[n, sl, :] * jnp.concatenate([fade, fade], 1) + jnp.dot(
                w.astype(BF), values, preferred_element_type=F32
            )
            peak[n, sl, :] = now
            if after:
                after(sl)

    def attend_page(n, p, after=None):
        live = jnp.sum(jnp.where(page_number == p, lens[...], 0).astype(F32), axis=1, keepdims=True)
        attend(n, kv.at[p], jnp.where(slab_row < live, 0.0, floor_value), after)

    def attend_fresh(n, home, first, count):
        count *= fresh
        at = pl.ds(pl.multiple_of(first * fresh, fresh), count)
        row = lax.broadcasted_iota(jnp.int32, (fresh, count), 1) + first * fresh
        position = lax.broadcasted_iota(jnp.int32, (fresh, count), 0) + home * fresh
        attend(n, kv_fresh.at[at], jnp.where(row <= position, 0.0, floor_value))

    own_page.wait()
    for c in order_right:
        split(ci, c)
    attend_page(0, ci)

    depth = next(n for n in (256, 128, 64, 32, 16) if width % n == 0)
    copies_w[1].wait()

    def unpack(i, carry):
        at = pl.ds(pl.multiple_of(i * depth, depth), depth)
        block = pltpu.einshape("dgh->gdh", wi[at])
        wg[at, :] = block[0]
        wu[at, :] = block[1]
        return carry

    lax.fori_loop(0, width // depth, unpack, 0)

    @pl.when(inner)
    def _():
        pl.semaphore_wait(entered.at[1], 1)
        tell(2, near_edge)
        send_small(far_edge)

    @pl.when(edge)
    def _():
        pl.semaphore_wait(entered.at[2], 1)
        send_small(last - beside_edge)
        send_small(far_edge)

    for c in inputs[2:]:
        c.wait()
    ids_all[ci] = ids[...]
    scores_all[ci] = scores[...]

    def route():
        others = pl.ds(0, last)
        remote(ids_all.at[others], ids_all.at[others], ids_s.at[0], ids_r.at[0], ctx_peer(1)).wait_recv()
        remote(scores_all.at[others], scores_all.at[others], sc_s.at[0], sc_r.at[0], ctx_peer(1)).wait_recv()
        lanes = exp_count * capacity
        lane = lax.broadcasted_iota(jnp.int32, (lanes, rows), 0)
        wanted = ci * exp_count + lax.rem(ei + lane // capacity, exp_count)
        seat = (lane - lane // capacity * capacity).astype(F32)
        earlier = (
            lax.broadcasted_iota(jnp.int32, (rows, rows), 0)
            < lax.broadcasted_iota(jnp.int32, (rows, rows), 1)
        ).astype(F32)
        for k in range(ctx_count):
            given = scores_all[k]
            combine_all[k] = (given / jnp.sum(given, axis=0, keepdims=True)).astype(BF).astype(F32)
        for k in range(ctx_count):
            chosen = jnp.zeros((lanes, rows), F32)
            portion = jnp.zeros((lanes, rows), F32)
            for j in range(top):
                hit = ids_all[k, j:j + 1, :] == wanted
                chosen = jnp.where(hit, 1.0, chosen)
                portion = jnp.where(hit, combine_all[k, j:j + 1, :], portion)
            rank = jnp.dot(chosen.astype(BF), earlier.astype(BF), preferred_element_type=F32)
            seated = (chosen > 0.5) & (rank == seat)
            place[k] = jnp.where(seated, 1.0, 0.0)
            gather[k] = jnp.where(seated, portion, 0.0)

    def arrive(p, c):
        piece(p, c, raw.at[p], 0, 1).wait_recv()

    def pass_on(c):
        @pl.when(ci < across)
        def _():
            piece(near_edge, c, raw.at[near_edge], 2, 1).start()

        if c < halves:
            @pl.when(ci > across)
            def _():
                piece(near_edge, c, raw.at[near_edge], 2, -1).start()

    def arrive_fresh(p):
        arrive(p, halves)
        split(p, halves)

    block_rows = stacked // level_send.shape[0]

    def part_copy(sl, where):
        return remote(part_send.at[sl], part_recv.at[sl], part_sem.at[0], part_sem.at[1], {"ctx": where})

    def level_copy(where):
        return remote(level_send, level_recv, part_sem.at[2], part_sem.at[3], {"ctx": where})

    @pl.when(inner)
    def _():
        @pl.when(ci < across)
        def _():
            arrive(near_edge, halves)
            pass_on(halves)
            split(near_edge, halves)

        @pl.when(ci > across)
        def _():
            arrive_fresh(across)

        for c in range(halves):
            arrive(near_edge, c)
            pass_on(c)
            split(near_edge, c)
            arrive(across, c)
            split(across, c)
        attend_page(0, near_edge)
        attend_page(0, across)
        query_copy(ci).wait_recv()
        stage_queries(1)
        attend_page(1, across)

        @pl.when(ci > across)
        def _():
            arrive_fresh(far_edge)
            attend_fresh(1, near_edge, 0, ctx_count // 2)

        attend_fresh(0, ci, 0, ctx_count)
        route()
        for c in range(halves):
            arrive(far_edge, c)
            split(far_edge, c)

        def finish(sl):
            for b in range(sl.start // block_rows, sl.stop // block_rows):
                at = slice(b * block_rows, (b + 1) * block_rows)
                whole = accum[1, at, HEAD:]
                part_send[at, :] = (accum[1, at, :HEAD] / whole).astype(BF)
                level = peak[1, at, :] * scaling + jnp.log(whole) * 1.4426950408889634
                level_send[b:b + 1, :] = jnp.transpose(level)[:1, :]
            part_copy(sl, near_edge).start()

        attend_page(1, far_edge, finish)
        level_copy(near_edge).start()
        attend_page(0, far_edge)
        for h in range(heads):
            sl = slice(h * fresh, (h + 1) * fresh)
            context_out[:, h * HEAD:(h + 1) * HEAD] = (accum[0, sl, :HEAD] / accum[0, sl, HEAD:]).astype(BF)

    @pl.when(edge)
    def _():
        @pl.when(ci > 0)
        def _():
            arrive_fresh(beside_edge)

        attend_fresh(0, ci, jnp.where(ci == 0, 0, ctx_count // 2), ctx_count // 2)
        for c in range(halves):
            arrive(beside_edge, c)
            split(beside_edge, c)
        attend_page(0, beside_edge)
        route()
        part_copy(slice(0, stacked), ci).wait_recv()
        level_copy(ci).wait_recv()
        per = block_rows // fresh
        for b in range(stacked // block_rows):
            sl = slice(b * block_rows, (b + 1) * block_rows)
            theirs = jnp.transpose(jnp.broadcast_to(level_recv[b:b + 1, :], (HEAD, block_rows)))
            ours = peak[0, sl, :] * scaling
            level = jnp.maximum(ours, theirs)
            fade = jnp.exp2(ours - level)
            share = jnp.exp2(theirs - level)
            merged = (accum[0, sl, :HEAD] * fade + part_recv[sl, :].astype(F32) * share) / (
                accum[0, sl, HEAD:] * fade + share
            )
            for h in range(per):
                at = b * per + h
                context_out[:, at * HEAD:(at + 1) * HEAD] = merged[h * fresh:(h + 1) * fresh, :].astype(BF)

    copies_w[0].wait()

    pieces = 4
    piece_width = width // pieces
    senders = pl.ds(1, exp_count - 1)
    for n in range(pieces):
        cols = slice(n * piece_width, (n + 1) * piece_width)
        part = jnp.dot(context_out[...], wo[:, cols], preferred_element_type=F32)
        rs_full[n] = part
        for k in range(1, exp_count):
            at = pl.ds(pl.multiple_of(lax.rem(ei + k, exp_count) * rows, rows), rows)
            rs_send[k, n] = rs_full[n, at, :].astype(BF)
            remote(rs_send.at[k, n], rs_recv.at[k, n], rs_s.at[0], rs_r.at[n], exp_peer(k)).start()
    mine = pl.ds(pl.multiple_of(ei * rows, rows), rows)
    square = jnp.zeros((rows, 1), F32)
    for n in range(pieces):
        cols = slice(n * piece_width, (n + 1) * piece_width)
        share = rs_full[n, mine, :]
        remote(rs_send.at[senders, n], rs_recv.at[senders, n], rs_s.at[0], rs_r.at[n], exp_peer(1)).wait_recv()
        for k in range(1, exp_count):
            share = share + rs_recv[k, n].astype(F32)
        h = (residual[:, cols].astype(F32) + share).astype(BF)
        hidden[:, cols] = h
        wide = h.astype(F32)
        square = square + jnp.sum(wide * wide, axis=1, keepdims=True)
    inverse = lax.rsqrt(square / width + norm_epsilon)
    nz[ci] = (hidden[...].astype(F32) * inverse * gain[...]).astype(BF)

    middle = last / 2
    send_table, work_table = [], []
    for c in range(ctx_count):
        others = [p for p in range(ctx_count) if p != c]
        send_table.append(sorted(others, key=lambda p: (abs(p - c) % last, abs(p - middle))))
        work_table.append([c] + sorted(others, key=lambda p: ((abs(p - c) - 1) % (last - 1) if last > 1 else 0, abs(p - middle))))

    def lookup(table, n):
        value = jnp.int32(table[0][n])
        for c in range(1, ctx_count):
            value = jnp.where(ci == c, table[c][n], value)
        return value

    def nz_copy(p, where):
        return remote(nz.at[p], nz.at[p], nz_s.at[0], nz_r.at[p], {"ctx": where})

    for n in range(last):
        nz_copy(ci, lookup(send_table, n)).start()

    places = [lookup(work_table, n) for n in range(ctx_count)]

    def dx_copy(j, n):
        p = places[n]
        return remote(x_send.at[j, p], x_recv.at[j, p], dx_s.at[0], dx_r.at[p], exp_peer(1 if j is senders else j))

    def ret_copy(j, n):
        p = places[n]
        return remote(y_send.at[j, p], y_recv.at[j, p], ret_s.at[0], ret_r.at[p], exp_peer(1 if j is senders else exp_count - j))

    def mix_copy(n):
        p = places[n]
        return remote(mix_send.at[p], mix_recv.at[ci], mix_s.at[0], mix_r.at[ci], {"ctx": p})

    def dispatch(n):
        p = places[n]
        if n:
            nz_copy(p, p).wait_recv()
        routed = jnp.dot(place[p].astype(BF), nz[p], preferred_element_type=F32)
        for j in list(range(1, exp_count)) + [0]:
            block = routed[j * capacity:(j + 1) * capacity].astype(BF)
            if j == 0:
                x_recv[0, p] = block
            else:
                x_send[j, p] = block
                dx_copy(j, n).start()

    def experts(n):
        p = places[n]
        dx_copy(senders, n).wait_recv()
        x = jnp.concatenate([x_recv[j, p].astype(F32) for j in range(exp_count)], 0).astype(BF)
        gate = jnp.dot(x, wg[...], preferred_element_type=F32)
        up = jnp.dot(x, wu[...], preferred_element_type=F32)
        act = (gate / (1.0 + jnp.exp(-gate)) * up).astype(BF)
        result = jnp.dot(act, wd[...], preferred_element_type=F32)
        for j in list(range(1, exp_count)) + [0]:
            block = result[j * capacity:(j + 1) * capacity].astype(BF)
            if j == 0:
                y_recv[0, p] = block
            else:
                y_send[j, p] = block
                ret_copy(j, n).start()

    def mixing(n):
        p = places[n]
        ret_copy(senders, n).wait_recv()
        rows_p = jnp.concatenate([y_recv[j, p].astype(F32) for j in range(exp_count)], 0).astype(BF)
        mixed = lax.dot_general(
            gather[p].astype(BF), rows_p, (((0,), (0,)), ((), ())), preferred_element_type=F32
        )
        if n == 0:
            return mixed
        mix_send[p] = mixed.astype(BF)
        mix_copy(n).start()

    dispatch(0)
    dispatch(1)
    copies_w[2].wait()
    experts(0)
    pl.when(inner)(lambda: experts(1))
    dispatch(2)
    dispatch(3)
    pl.when(edge)(lambda: experts(1))
    experts(2)
    mixing(1)
    experts(ctx_count - 1)
    for n in range(max(1, ctx_count - 2), ctx_count):
        mixing(n)
    out = hidden[...].astype(F32) + mixing(0)
    for n in range(1, ctx_count):
        p = places[n]
        remote(mix_send.at[p], mix_recv.at[p], mix_s.at[0], mix_r.at[p], {"ctx": p}).wait_recv()
        out = out + mix_recv[p].astype(F32)
    layer_out[...] = out.astype(BF)

    others = pl.ds(0, last)
    for src, dst, sem in [
        (ids_all.at[others], ids_all.at[others], ids_s), (scores_all.at[others], scores_all.at[others], sc_s),
        (nz.at[others], nz.at[others], nz_s), (mix_send.at[others], mix_recv.at[others], mix_s),
    ]:
        remote(src, dst, sem.at[0], mix_r.at[0], ctx_peer(1)).wait_send()
    for src, dst, sem in [
        (rs_send.at[senders], rs_recv.at[senders], rs_s), (x_send.at[senders], x_recv.at[senders], dx_s),
        (y_send.at[senders], y_recv.at[senders], ret_s),
    ]:
        remote(src, dst, sem.at[0], mix_r.at[0], exp_peer(1)).wait_send()

    everything = pl.ds(0, slab + fresh)
    cached = pl.ds(0, slab)

    def sent(at, sem):
        remote(raw.at[0, at], raw.at[0, at], kv_send.at[sem], kv_recv.at[0, 0], ctx_peer(1)).wait_send()

    @pl.when(ci < last)
    def _():
        sent(everything, 0)

    @pl.when(ci > 0)
    def _():
        sent(cached, 1)

    @pl.when(edge)
    def _():
        query_copy(beside_edge).wait_send()

    @pl.when(inner)
    def _():
        @pl.when(ci < across)
        def _():
            sent(everything, 2)

        @pl.when(ci > across)
        def _():
            sent(cached, 2)

        part_copy(slice(0, stacked), near_edge).wait_send()
        level_copy(near_edge).wait_send()


def settle(context, layer, context_out, layer_out, sem):
    copies = [
        pltpu.make_async_copy(context, context_out, sem.at[0]),
        pltpu.make_async_copy(layer, layer_out, sem.at[1]),
    ]
    for c in copies:
        c.start()
    for c in copies:
        c.wait()


def fused_device(
    ctx_count, exp_count, queries, pages, cached_lengths, residual_in, out_weight, norm_gain,
    expert_ids, route_scores, expert_input, expert_output,
):
    fresh, query_width = queries.shape[1:]
    page_size = pages.shape[1]
    slab = page_size - fresh
    rows, width = residual_in.shape[1:]
    top = expert_ids.shape[2]
    hidden_width = expert_input.shape[3]
    experts = ctx_count * exp_count
    capacity = max(2, -(-rows * top // experts))
    stacked = query_width // HEAD * fresh
    vm = pl.BlockSpec(memory_space=pltpu.VMEM)
    hbm = pl.BlockSpec(memory_space=pl.ANY)
    dma = pltpu.SemaphoreType.DMA
    V = pltpu.VMEM
    lanes = exp_count * capacity
    pieces = 4
    halves = 2 if slab % 32 == 0 else 1
    blocks = stacked // HEAD
    context, layer_out = pl.pallas_call(
        functools.partial(fused_kernel, ctx_count, exp_count, capacity),
        out_shape=(V((fresh, query_width), BF), V((rows, width), BF)),
        in_specs=[hbm] * 10,
        out_specs=(vm, vm),
        scratch_shapes=[
            V((1, ctx_count), jnp.int32),
            V((2, fresh, query_width), BF),
            V((rows, width), BF),
            V((1, width), F32),
            V((top, rows), jnp.int32),
            V((top, rows), F32),
            V((ctx_count,) + pages.shape[1:], BF),
            V((ctx_count, slab, 3 * HEAD), BF),
            V((ctx_count * fresh, 3 * HEAD), BF),
            V((2, stacked, HEAD), BF),
            V((2, stacked, HEAD), F32),
            V((2, stacked, 2 * HEAD), F32),
            V((stacked, HEAD), BF),
            V((stacked, HEAD), BF),
            V((blocks, HEAD), F32),
            V((blocks, HEAD), F32),
            V(out_weight.shape, BF),
            V(expert_input.shape[1:], BF),
            V((width, hidden_width), BF),
            V((width, hidden_width), BF),
            V(expert_output.shape[1:], BF),
            V((ctx_count, top, rows), jnp.int32),
            V((ctx_count, top, rows), F32),
            V((ctx_count, top, rows), F32),
            V((ctx_count, lanes, rows), F32),
            V((ctx_count, lanes, rows), F32),
            V((pieces, fresh, width // pieces), F32),
            V((exp_count, pieces, rows, width // pieces), BF),
            V((exp_count, pieces, rows, width // pieces), BF),
            V((rows, width), BF),
            V((ctx_count, rows, width), BF),
            V((exp_count, ctx_count, capacity, width), BF),
            V((exp_count, ctx_count, capacity, width), BF),
            V((exp_count, ctx_count, capacity, width), BF),
            V((exp_count, ctx_count, capacity, width), BF),
            V((ctx_count, rows, width), BF),
            V((ctx_count, rows, width), BF),
            dma((1,)), dma((6,)), dma((3,)), dma((ctx_count, halves + 1)), dma((3,)), dma((2,)), dma((4,)),
            pltpu.SemaphoreType.REGULAR((3,)),
            dma((1,)), dma((1,)), dma((1,)), dma((1,)), dma((1,)), dma((pieces,)), dma((1,)), dma((ctx_count,)),
            dma((1,)), dma((ctx_count,)), dma((1,)), dma((ctx_count,)), dma((1,)), dma((ctx_count,)),
        ],
        compiler_params=pltpu.CompilerParams(
            collective_id=0, has_side_effects=True, vmem_limit_bytes=VMEM_LIMIT
        ),
    )(
        cached_lengths, queries[0], pages[0], residual_in[0], norm_gain.reshape(1, width),
        expert_ids[0].T, route_scores[0].T, out_weight, expert_input[0], expert_output[0],
    )
    context, layer_out = pl.pallas_call(
        settle,
        out_shape=(
            jax.ShapeDtypeStruct(context.shape, BF),
            jax.ShapeDtypeStruct(layer_out.shape, BF),
        ),
        in_specs=[vm, vm],
        out_specs=(hbm, hbm),
        scratch_shapes=[dma((2,))],
    )(
        pltpu.with_memory_space_constraint(context, pltpu.VMEM),
        pltpu.with_memory_space_constraint(layer_out, pltpu.VMEM),
    )
    return context[None], layer_out[None]


def fused_fits(mesh):
    return mesh.shape["rep"] == 1 and mesh.shape["ctx"] == 4


def solution(mesh):
    in_specs = (
        P("groups", "ctx", ("exp", "rep")),
        P("groups", "ctx", None, "exp"),
        P("groups", None),
        P("groups", ("ctx", "exp"), None),
        P(("exp", "rep"), None),
        P(),
        P("groups", ("ctx", "exp"), None),
        P("groups", ("ctx", "exp"), None),
        P(("ctx", "exp"), None, None, "rep"),
        P(("ctx", "exp"), "rep", None),
    )
    out_specs = (P("groups", "ctx", ("exp", "rep")), P("groups", ("ctx", "exp", "rep"), None))
    body = per_device
    if fused_fits(mesh):
        body = functools.partial(fused_device, mesh.shape["ctx"], mesh.shape["exp"])
    return jax.shard_map(
        body, mesh=mesh, in_specs=in_specs, out_specs=out_specs, check_vma=False
    )
```

```python
import functools

import jax
import jax.numpy as jnp
from jax import lax
from jax.experimental import pallas as pl
from jax.experimental.pallas import tpu as pltpu
from jax.sharding import PartitionSpec as P

HEAD = 128


floor_value = -1e30
norm_epsilon = 1e-06


def normalize(hidden, norm_gain):
    widened = hidden.astype(jnp.float32)
    mean_square = jnp.mean(widened * widened, axis=-1, keepdims=True)
    return (widened * lax.rsqrt(mean_square + norm_epsilon) * norm_gain).astype(jnp.bfloat16)


def attend_piece(query_rows, page_rows, allowed):
    scaling = query_rows.shape[-1] ** (-0.5)
    scores = (
        jnp.einsum(
            "rqhe,rke->rqhk", query_rows, page_rows[:, :, 0], preferred_element_type=jnp.float32
        )
        * scaling
    )
    permitted = allowed[:, :, None, :]
    masked = jnp.where(permitted, scores, floor_value)
    peaks = jnp.max(masked, axis=-1)
    weights = jnp.where(permitted, jnp.exp(masked - peaks[..., None]), 0.0)
    totals = jnp.sum(weights, axis=-1)
    summed = jnp.einsum(
        "rqhk,rke->rqhe",
        weights.astype(jnp.bfloat16),
        page_rows[:, :, 1],
        preferred_element_type=jnp.float32,
    )
    return (peaks, totals, summed)


def merge_partials(earlier, later):
    peaks = jnp.maximum(earlier[0], later[0])
    later_scale = jnp.exp(later[0] - peaks)
    totals = later[1] * later_scale
    summed = later[2] * later_scale[..., None]
    return (peaks, totals, summed)


def rows_mask(row_index, lengths, query_positions, slab_size, fresh_block):
    page_size = slab_size + fresh_block
    page_number = row_index // page_size
    offset = row_index - page_number * page_size
    page_count = lengths.shape[1]
    picker = page_number[None, :] == jnp.arange(page_count, dtype=jnp.int32)[:, None]
    live_length = jnp.sum(jnp.where(picker[None], lengths[:, :, None], 0), axis=1)
    in_cache = (offset < slab_size)[None, :] & (offset[None, :] < live_length)
    fresh_position = page_number * fresh_block + offset - slab_size
    in_fresh = (offset >= slab_size)[None, :] & (
        fresh_position[None, :] <= query_positions[:, None]
    )
    return in_cache[:, None, :] | in_fresh[None, :, :]


def per_device(
    queries,
    pages,
    cached_lengths,
    residual_in,
    out_weight,
    norm_gain,
    expert_ids,
    route_scores,
    expert_input,
    expert_output,
):
    requests, fresh_block, query_width = queries.shape
    local_heads = query_width // HEAD
    core_place = lax.axis_index("rep")
    page_place = lax.axis_index("ctx")
    rep_count = lax.axis_size("rep")
    page_size = pages.shape[1]
    slab_size = page_size - fresh_block
    own_positions = page_place * fresh_block + jnp.arange(fresh_block, dtype=jnp.int32)
    query_rows = queries.reshape(requests, fresh_block, local_heads, HEAD)
    start_state = (
        jnp.full((requests, fresh_block, local_heads), floor_value, jnp.float32),
        jnp.zeros((requests, fresh_block, local_heads), jnp.float32),
        jnp.zeros((requests, fresh_block, local_heads, HEAD), jnp.float32),
    )
    page_piece = lax.all_gather(pages, "ctx", axis=1, tiled=True)
    row_index = jnp.arange(page_piece.shape[1], dtype=jnp.int32)
    allowed = rows_mask(row_index, cached_lengths, own_positions, slab_size, fresh_block)
    peaks, totals, summed = merge_partials(
        start_state, attend_piece(query_rows, page_piece, allowed)
    )
    context = (
        (summed / totals[..., None])
        .astype(jnp.bfloat16)
        .reshape(requests, fresh_block, query_width)
    )
    projected = jnp.dot(
        context.reshape(requests * fresh_block, query_width),
        out_weight,
        preferred_element_type=jnp.float32,
    ).reshape(requests, fresh_block, -1)
    token_block = residual_in.shape[1]
    share_size = token_block // rep_count
    own_share = lax.psum_scatter(
        projected.astype(jnp.bfloat16), ("exp", "rep"), scatter_dimension=1, tiled=True
    ).astype(jnp.float32)
    own_residual = lax.dynamic_slice_in_dim(residual_in, core_place * share_size, share_size, 1)
    own_hidden = (own_residual.astype(jnp.float32) + own_share).astype(jnp.bfloat16)
    normed = lax.all_gather(normalize(own_hidden, norm_gain), "rep", axis=1, tiled=True)
    top_count = expert_ids.shape[2]
    expert_count = lax.axis_size("ctx") * lax.axis_size("exp")
    most_rows = max(2, (token_block * top_count + expert_count - 1) // expert_count)
    capacity = requests * most_rows
    model_width = normed.shape[2]
    token_count = requests * token_block
    flat_ids = expert_ids.reshape(-1)
    row_count = flat_ids.shape[0]
    chosen = (flat_ids[:, None] == jnp.arange(expert_count, dtype=jnp.int32)[None, :]).astype(
        jnp.int32
    )
    earlier_rows = jnp.cumsum(chosen, axis=0) - chosen
    slot_rank = jnp.sum(earlier_rows * chosen, axis=1)
    slot_index = flat_ids * capacity + slot_rank
    slot_onehot = (
        slot_index[:, None] == jnp.arange(expert_count * capacity, dtype=jnp.int32)[None, :]
    ).astype(jnp.bfloat16)
    token_onehot = (
        (jnp.arange(row_count, dtype=jnp.int32) // top_count)[:, None]
        == jnp.arange(token_count, dtype=jnp.int32)[None, :]
    ).astype(jnp.bfloat16)
    placement = jnp.dot(slot_onehot.T, token_onehot, preferred_element_type=jnp.float32).astype(
        jnp.bfloat16
    )
    outgoing = jnp.dot(
        placement, normed.reshape(token_count, model_width), preferred_element_type=jnp.float32
    )
    outgoing = outgoing.astype(jnp.bfloat16).reshape(expert_count, capacity, model_width)
    scores_sum = jnp.sum(route_scores, axis=2, keepdims=True)
    combine = (route_scores / scores_sum).astype(jnp.bfloat16).reshape(-1)
    gathering = jnp.dot(
        (token_onehot * combine[:, None]).T, slot_onehot, preferred_element_type=jnp.float32
    ).astype(jnp.bfloat16)
    gate_up = expert_input[0]
    down_weight = expert_output[0]
    arrived_rows = lax.all_to_all(outgoing, ("ctx", "exp"), split_axis=0, concat_axis=0, tiled=True)
    inner_rows = jnp.einsum(
        "nd,dgh->ngh",
        arrived_rows.reshape(-1, model_width),
        gate_up,
        preferred_element_type=jnp.float32,
    )
    activated = (jax.nn.silu(inner_rows[:, 0]) * inner_rows[:, 1]).astype(jnp.bfloat16)
    result = jnp.dot(activated, down_weight, preferred_element_type=jnp.float32).astype(
        jnp.bfloat16
    )
    returned = lax.all_to_all(
        result.reshape(arrived_rows.shape), ("ctx", "exp"), split_axis=0, concat_axis=0, tiled=True
    )
    mixture = jnp.dot(
        gathering,
        returned.reshape(expert_count * capacity, model_width),
        preferred_element_type=jnp.float32,
    )
    own_mixture = lax.psum_scatter(
        mixture.reshape(requests, token_block, model_width).astype(jnp.bfloat16),
        "rep",
        scatter_dimension=1,
        tiled=True,
    ).astype(jnp.float32)
    layer_out = (own_hidden.astype(jnp.float32) + own_mixture).astype(jnp.bfloat16)
    return (context, layer_out)


BF = jnp.bfloat16
F32 = jnp.float32
MESH = pl.DeviceIdType.MESH
VMEM_LIMIT = 60 * 1024 * 1024


def fused_kernel(
    ctx_count, exp_count, capacity,
    lengths, query, page, residual_in, gain_in, ids_in, scores_in, w_out, w_in, w_down,
    context_out, layer_out,
    lens, q_in, residual, gain, ids, scores,
    raw, kv, kv_fresh, q_rows, peak, accum, part_send, part_recv, level_send, level_recv,
    wo, wi, wg, wu, wd,
    ids_all, scores_all, combine_all, place, gather,
    rs_full, rs_send, rs_recv, hidden, nz, x_send, x_recv, y_send, y_recv, mix_send, mix_recv,
    own_sem, in_sem, kv_send, kv_recv, w_sem, q_sem, part_sem, entered,
    ids_s, ids_r, sc_s, sc_r, rs_s, rs_r, nz_s, nz_r, dx_s, dx_r, ret_s, ret_r, mix_s, mix_r,
):
    ci = lax.axis_index("ctx")
    ei = lax.axis_index("exp")
    fresh = q_in.shape[1]
    heads = q_in.shape[2] // HEAD
    slab = kv.shape[1]
    halves = 2 if slab % 32 == 0 else 1
    half_rows = slab // halves
    rows = residual.shape[0]
    width = residual.shape[1]
    top = ids.shape[0]
    stacked = q_rows.shape[1]
    scaling = HEAD ** (-0.5) * 1.4426950408889634

    last = ctx_count - 1
    edge = (ci == 0) | (ci == last)
    inner = (ci > 0) & (ci < last)
    near_edge = jnp.where(ci < 2, 0, last)
    across = last - ci
    far_edge = last - near_edge
    beside_edge = jnp.where(ci == 0, 1, last - 1)

    def ctx_peer(k):
        return {"ctx": lax.rem(ci + k, ctx_count)}

    def exp_peer(k):
        return {"exp": lax.rem(ei + k, exp_count)}

    def remote(src, dst, ss, rs, where):
        return pltpu.make_async_remote_copy(
            src_ref=src, dst_ref=dst, send_sem=ss, recv_sem=rs, device_id=where, device_id_type=MESH
        )

    barrier = pltpu.get_barrier_semaphore()

    @pl.when(inner)
    def _():
        for where in (across, near_edge):
            pl.semaphore_signal(barrier, inc=1, device_id={"ctx": where}, device_id_type=MESH)

    for k in range(1, exp_count):
        pl.semaphore_signal(barrier, inc=1, device_id=exp_peer(k), device_id_type=MESH)

    def tell(n, where):
        pl.semaphore_signal(entered.at[n], inc=1, device_id={"ctx": where}, device_id_type=MESH)

    own_page = pltpu.make_async_copy(page, raw.at[ci], own_sem.at[0])
    own_page.start()
    inputs = [
        pltpu.make_async_copy(src, dst, in_sem.at[n])
        for n, (src, dst) in enumerate(
            [(lengths, lens), (query, q_in.at[0]), (residual_in, residual), (gain_in, gain), (ids_in, ids), (scores_in, scores)]
        )
    ]
    for c in inputs:
        c.start()
    copies_w = [
        pltpu.make_async_copy(w_out, wo, w_sem.at[0]),
        pltpu.make_async_copy(w_in, wi, w_sem.at[1]),
        pltpu.make_async_copy(w_down, wd, w_sem.at[2]),
    ]
    for n in (1, 0, 2):
        copies_w[n].start()

    kv[:, :, 2 * HEAD:] = jnp.ones(kv.shape[:2] + (HEAD,), BF)
    kv_fresh[:, :2 * HEAD] = jnp.zeros((kv_fresh.shape[0], 2 * HEAD), BF)
    kv_fresh[:, 2 * HEAD:] = jnp.ones((kv_fresh.shape[0], HEAD), BF)
    accum[...] = jnp.zeros_like(accum)
    peak[...] = jnp.full_like(peak, floor_value)
    pl.semaphore_wait(barrier, exp_count)

    def send_small(where):
        remote(ids_in, ids_all.at[ci], ids_s.at[0], ids_r.at[0], {"ctx": where}).start()
        remote(scores_in, scores_all.at[ci], sc_s.at[0], sc_r.at[0], {"ctx": where}).start()

    def rows_of(c):
        return pl.ds(c * half_rows, half_rows) if c < halves else pl.ds(slab, fresh)

    def piece(p, c, src, sem, step):
        return remote(src.at[rows_of(c)], raw.at[p, rows_of(c)], kv_send.at[sem], kv_recv.at[p, c], {"ctx": ci + step})

    order_right = [halves] + list(range(halves))
    order_left = list(range(halves))

    def send_right():
        for c in order_right:
            piece(ci, c, page, 0, 1).start()

    def send_left():
        for c in order_left:
            piece(ci, c, page, 1, -1).start()

    def query_copy(where):
        return remote(query, q_in.at[1], q_sem.at[0], q_sem.at[1], {"ctx": where})

    @pl.when(edge)
    def _():
        tell(0, beside_edge)
        send_small(beside_edge)

        @pl.when(ci == 0)
        def _():
            send_right()

        @pl.when(ci > 0)
        def _():
            send_left()

        query_copy(beside_edge).start()

    @pl.when(inner)
    def _():
        send_small(across)

        @pl.when(ci < across)
        def _():
            send_right()

        @pl.when(ci > across)
        def _():
            send_left()

        pl.semaphore_wait(entered.at[0], 1)
        tell(1, across)
        send_small(near_edge)

        @pl.when(ci < across)
        def _():
            send_left()

        @pl.when(ci > across)
        def _():
            send_right()

    def stage_queries(n):
        for h in range(heads):
            q_rows[n, h * fresh:(h + 1) * fresh, :] = q_in[n, :, h * HEAD:(h + 1) * HEAD]

    inputs[0].wait()
    inputs[1].wait()
    stage_queries(0)

    step = next(n for n in (4, 2, 1) if heads % n == 0)
    page_number = lax.broadcasted_iota(jnp.int32, (1, ctx_count), 1)
    slab_row = lax.broadcasted_iota(jnp.int32, (1, slab), 1).astype(F32)

    def split(p, c):
        both = pltpu.einshape("sgh->gsh", raw[p, rows_of(c)])
        if c < halves:
            kv[p, rows_of(c), :HEAD] = both[0]
            kv[p, rows_of(c), HEAD:2 * HEAD] = both[1]
        else:
            at = pl.ds(pl.multiple_of(p * fresh, fresh), fresh)
            kv_fresh[at, :HEAD] = both[0]
            kv_fresh[at, HEAD:2 * HEAD] = both[1]

    def attend(n, source, bias, after=None):
        keys = source[:, :HEAD]
        values = source[:, HEAD:]
        count = keys.shape[0]
        for h in range(0, heads, step):
            sl = slice(h * fresh, (h + step) * fresh)
            s = lax.dot_general(
                q_rows[n, sl, :], keys, (((1,), (1,)), ((), ())), preferred_element_type=F32
            )
            s = (s.reshape(step, fresh, count) + bias[None]).reshape(step * fresh, count)
            old = peak[n, sl, :]
            now = jnp.maximum(old, jnp.max(s, axis=1, keepdims=True))
            w = jnp.exp2((s - now[:, :1]) * scaling)
            fade = jnp.exp2((old - now) * scaling)
            accum[n, sl, :] = accum[n, sl, :] * jnp.concatenate([fade, fade], 1) + jnp.dot(
                w.astype(BF), values, preferred_element_type=F32
            )
            peak[n, sl, :] = now
            if after:
                after(sl)

    def attend_page(n, p, after=None):
        live = jnp.sum(jnp.where(page_number == p, lens[...], 0).astype(F32), axis=1, keepdims=True)
        attend(n, kv.at[p], jnp.where(slab_row < live, 0.0, floor_value), after)

    def attend_fresh(n, home, first, count):
        count *= fresh
        at = pl.ds(pl.multiple_of(first * fresh, fresh), count)
        row = lax.broadcasted_iota(jnp.int32, (fresh, count), 1) + first * fresh
        position = lax.broadcasted_iota(jnp.int32, (fresh, count), 0) + home * fresh
        attend(n, kv_fresh.at[at], jnp.where(row <= position, 0.0, floor_value))

    own_page.wait()
    for c in order_right:
        split(ci, c)
    attend_page(0, ci)

    depth = next(n for n in (256, 128, 64, 32, 16) if width % n == 0)
    copies_w[1].wait()

    def unpack(i, carry):
        at = pl.ds(pl.multiple_of(i * depth, depth), depth)
        block = pltpu.einshape("dgh->gdh", wi[at])
        wg[at, :] = block[0]
        wu[at, :] = block[1]
        return carry

    lax.fori_loop(0, width // depth, unpack, 0)

    @pl.when(inner)
    def _():
        pl.semaphore_wait(entered.at[1], 1)
        tell(2, near_edge)
        send_small(far_edge)

    @pl.when(edge)
    def _():
        pl.semaphore_wait(entered.at[2], 1)
        send_small(last - beside_edge)
        send_small(far_edge)

    for c in inputs[2:]:
        c.wait()
    ids_all[ci] = ids[...]
    scores_all[ci] = scores[...]

    def route():
        others = pl.ds(0, last)
        remote(ids_all.at[others], ids_all.at[others], ids_s.at[0], ids_r.at[0], ctx_peer(1)).wait_recv()
        remote(scores_all.at[others], scores_all.at[others], sc_s.at[0], sc_r.at[0], ctx_peer(1)).wait_recv()
        lanes = exp_count * capacity
        lane = lax.broadcasted_iota(jnp.int32, (lanes, rows), 0)
        wanted = ci * exp_count + lax.rem(ei + lane // capacity, exp_count)
        seat = (lane - lane // capacity * capacity).astype(F32)
        earlier = (
            lax.broadcasted_iota(jnp.int32, (rows, rows), 0)
            < lax.broadcasted_iota(jnp.int32, (rows, rows), 1)
        ).astype(F32)
        for k in range(ctx_count):
            given = scores_all[k]
            combine_all[k] = (given / jnp.sum(given, axis=0, keepdims=True)).astype(BF).astype(F32)
        for k in range(ctx_count):
            chosen = jnp.zeros((lanes, rows), F32)
            portion = jnp.zeros((lanes, rows), F32)
            for j in range(top):
                hit = ids_all[k, j:j + 1, :] == wanted
                chosen = jnp.where(hit, 1.0, chosen)
                portion = jnp.where(hit, combine_all[k, j:j + 1, :], portion)
            rank = jnp.dot(chosen.astype(BF), earlier.astype(BF), preferred_element_type=F32)
            seated = (chosen > 0.5) & (rank == seat)
            place[k] = jnp.where(seated, 1.0, 0.0)
            gather[k] = jnp.where(seated, portion, 0.0)

    def arrive(p, c):
        piece(p, c, raw.at[p], 0, 1).wait_recv()

    def pass_on(c):
        @pl.when(ci < across)
        def _():
            piece(near_edge, c, raw.at[near_edge], 2, 1).start()

        if c < halves:
            @pl.when(ci > across)
            def _():
                piece(near_edge, c, raw.at[near_edge], 2, -1).start()

    def arrive_fresh(p):
        arrive(p, halves)
        split(p, halves)

    block_rows = stacked // level_send.shape[0]

    def part_copy(sl, where):
        return remote(part_send.at[sl], part_recv.at[sl], part_sem.at[0], part_sem.at[1], {"ctx": where})

    def level_copy(where):
        return remote(level_send, level_recv, part_sem.at[2], part_sem.at[3], {"ctx": where})

    @pl.when(inner)
    def _():
        @pl.when(ci < across)
        def _():
            arrive(near_edge, halves)
            pass_on(halves)
            split(near_edge, halves)

        @pl.when(ci > across)
        def _():
            arrive_fresh(across)

        for c in range(halves):
            arrive(near_edge, c)
            pass_on(c)
            split(near_edge, c)
            arrive(across, c)
            split(across, c)
        attend_page(0, near_edge)
        attend_page(0, across)
        query_copy(ci).wait_recv()
        stage_queries(1)
        attend_page(1, across)

        @pl.when(ci > across)
        def _():
            arrive_fresh(far_edge)
            attend_fresh(1, near_edge, 0, ctx_count // 2)

        attend_fresh(0, ci, 0, ctx_count)
        route()
        for c in range(halves):
            arrive(far_edge, c)
            split(far_edge, c)

        def finish(sl):
            for b in range(sl.start // block_rows, sl.stop // block_rows):
                at = slice(b * block_rows, (b + 1) * block_rows)
                whole = accum[1, at, HEAD:]
                part_send[at, :] = (accum[1, at, :HEAD] / whole).astype(BF)
                level = peak[1, at, :] * scaling + jnp.log(whole) * 1.4426950408889634
                level_send[b:b + 1, :] = jnp.transpose(level)[:1, :]
            part_copy(sl, near_edge).start()

        attend_page(1, far_edge, finish)
        level_copy(near_edge).start()
        attend_page(0, far_edge)
        for h in range(heads):
            sl = slice(h * fresh, (h + 1) * fresh)
            context_out[:, h * HEAD:(h + 1) * HEAD] = (accum[0, sl, :HEAD] / accum[0, sl, HEAD:]).astype(BF)

    @pl.when(edge)
    def _():
        @pl.when(ci > 0)
        def _():
            arrive_fresh(beside_edge)

        attend_fresh(0, ci, jnp.where(ci == 0, 0, ctx_count // 2), ctx_count // 2)
        for c in range(halves):
            arrive(beside_edge, c)
            split(beside_edge, c)
        attend_page(0, beside_edge)
        route()
        part_copy(slice(0, stacked), ci).wait_recv()
        level_copy(ci).wait_recv()
        per = block_rows // fresh
        for b in range(stacked // block_rows):
            sl = slice(b * block_rows, (b + 1) * block_rows)
            theirs = jnp.transpose(jnp.broadcast_to(level_recv[b:b + 1, :], (HEAD, block_rows)))
            ours = peak[0, sl, :] * scaling
            level = jnp.maximum(ours, theirs)
            fade = jnp.exp2(ours - level)
            share = jnp.exp2(theirs - level)
            merged = (accum[0, sl, :HEAD] * fade + part_recv[sl, :].astype(F32) * share) / (
                accum[0, sl, HEAD:] * fade + share
            )
            for h in range(per):
                at = b * per + h
                context_out[:, at * HEAD:(at + 1) * HEAD] = merged[h * fresh:(h + 1) * fresh, :].astype(BF)

    copies_w[0].wait()

    pieces = 4
    piece_width = width // pieces
    senders = pl.ds(1, exp_count - 1)
    for n in range(pieces):
        cols = slice(n * piece_width, (n + 1) * piece_width)
        part = jnp.dot(context_out[...], wo[:, cols], preferred_element_type=F32)
        rs_full[n] = part
        for k in range(1, exp_count):
            at = pl.ds(pl.multiple_of(lax.rem(ei + k, exp_count) * rows, rows), rows)
            rs_send[k, n] = rs_full[n, at, :].astype(BF)
            remote(rs_send.at[k, n], rs_recv.at[k, n], rs_s.at[0], rs_r.at[n], exp_peer(k)).start()
    mine = pl.ds(pl.multiple_of(ei * rows, rows), rows)
    square = jnp.zeros((rows, 1), F32)
    for n in range(pieces):
        cols = slice(n * piece_width, (n + 1) * piece_width)
        share = rs_full[n, mine, :]
        remote(rs_send.at[senders, n], rs_recv.at[senders, n], rs_s.at[0], rs_r.at[n], exp_peer(1)).wait_recv()
        for k in range(1, exp_count):
            share = share + rs_recv[k, n].astype(F32)
        h = (residual[:, cols].astype(F32) + share).astype(BF)
        hidden[:, cols] = h
        wide = h.astype(F32)
        square = square + jnp.sum(wide * wide, axis=1, keepdims=True)
    inverse = lax.rsqrt(square / width + norm_epsilon)
    nz[ci] = (hidden[...].astype(F32) * inverse * gain[...]).astype(BF)

    middle = last / 2
    send_table, work_table = [], []
    for c in range(ctx_count):
        others = [p for p in range(ctx_count) if p != c]
        send_table.append(sorted(others, key=lambda p: (abs(p - c) % last, abs(p - middle))))
        work_table.append([c] + sorted(others, key=lambda p: ((abs(p - c) - 1) % (last - 1) if last > 1 else 0, abs(p - middle))))

    def lookup(table, n):
        value = jnp.int32(table[0][n])
        for c in range(1, ctx_count):
            value = jnp.where(ci == c, table[c][n], value)
        return value

    def nz_copy(p, where):
        return remote(nz.at[p], nz.at[p], nz_s.at[0], nz_r.at[p], {"ctx": where})

    for n in range(last):
        nz_copy(ci, lookup(send_table, n)).start()

    places = [lookup(work_table, n) for n in range(ctx_count)]

    def dx_copy(j, n):
        p = places[n]
        return remote(x_send.at[j, p], x_recv.at[j, p], dx_s.at[0], dx_r.at[p], exp_peer(1 if j is senders else j))

    def ret_copy(j, n):
        p = places[n]
        return remote(y_send.at[j, p], y_recv.at[j, p], ret_s.at[0], ret_r.at[p], exp_peer(1 if j is senders else exp_count - j))

    def mix_copy(n):
        p = places[n]
        return remote(mix_send.at[p], mix_recv.at[ci], mix_s.at[0], mix_r.at[ci], {"ctx": p})

    def dispatch(n):
        p = places[n]
        if n:
            nz_copy(p, p).wait_recv()
        routed = jnp.dot(place[p].astype(BF), nz[p], preferred_element_type=F32)
        for j in list(range(1, exp_count)) + [0]:
            block = routed[j * capacity:(j + 1) * capacity].astype(BF)
            if j == 0:
                x_recv[0, p] = block
            else:
                x_send[j, p] = block
                dx_copy(j, n).start()

    def experts(n):
        p = places[n]
        dx_copy(senders, n).wait_recv()
        x = jnp.concatenate([x_recv[j, p].astype(F32) for j in range(exp_count)], 0).astype(BF)
        gate = jnp.dot(x, wg[...], preferred_element_type=F32)
        up = jnp.dot(x, wu[...], preferred_element_type=F32)
        act = (gate / (1.0 + jnp.exp(-gate)) * up).astype(BF)
        result = jnp.dot(act, wd[...], preferred_element_type=F32)
        for j in list(range(1, exp_count)) + [0]:
            block = result[j * capacity:(j + 1) * capacity].astype(BF)
            if j == 0:
                y_recv[0, p] = block
            else:
                y_send[j, p] = block
                ret_copy(j, n).start()

    def mixing(n):
        p = places[n]
        ret_copy(senders, n).wait_recv()
        rows_p = jnp.concatenate([y_recv[j, p].astype(F32) for j in range(exp_count)], 0).astype(BF)
        mixed = lax.dot_general(
            gather[p].astype(BF), rows_p, (((0,), (0,)), ((), ())), preferred_element_type=F32
        )
        if n == 0:
            return mixed
        mix_send[p] = mixed.astype(BF)
        mix_copy(n).start()

    dispatch(0)
    dispatch(1)
    copies_w[2].wait()
    experts(0)
    pl.when(inner)(lambda: experts(1))
    dispatch(2)
    dispatch(3)
    pl.when(edge)(lambda: experts(1))
    experts(2)
    experts(ctx_count - 1)
    for n in range(1, ctx_count):
        mixing(n)
    out = hidden[...].astype(F32) + mixing(0)
    for n in range(1, ctx_count):
        p = places[n]
        remote(mix_send.at[p], mix_recv.at[p], mix_s.at[0], mix_r.at[p], {"ctx": p}).wait_recv()
        out = out + mix_recv[p].astype(F32)
    layer_out[...] = out.astype(BF)

    others = pl.ds(0, last)
    for src, dst, sem in [
        (ids_all.at[others], ids_all.at[others], ids_s), (scores_all.at[others], scores_all.at[others], sc_s),
        (nz.at[others], nz.at[others], nz_s), (mix_send.at[others], mix_recv.at[others], mix_s),
    ]:
        remote(src, dst, sem.at[0], mix_r.at[0], ctx_peer(1)).wait_send()
    for src, dst, sem in [
        (rs_send.at[senders], rs_recv.at[senders], rs_s), (x_send.at[senders], x_recv.at[senders], dx_s),
        (y_send.at[senders], y_recv.at[senders], ret_s),
    ]:
        remote(src, dst, sem.at[0], mix_r.at[0], exp_peer(1)).wait_send()

    everything = pl.ds(0, slab + fresh)
    cached = pl.ds(0, slab)

    def sent(at, sem):
        remote(raw.at[0, at], raw.at[0, at], kv_send.at[sem], kv_recv.at[0, 0], ctx_peer(1)).wait_send()

    @pl.when(ci < last)
    def _():
        sent(everything, 0)

    @pl.when(ci > 0)
    def _():
        sent(cached, 1)

    @pl.when(edge)
    def _():
        query_copy(beside_edge).wait_send()

    @pl.when(inner)
    def _():
        @pl.when(ci < across)
        def _():
            sent(everything, 2)

        @pl.when(ci > across)
        def _():
            sent(cached, 2)

        part_copy(slice(0, stacked), near_edge).wait_send()
        level_copy(near_edge).wait_send()


def settle(context, layer, context_out, layer_out, sem):
    copies = [
        pltpu.make_async_copy(context, context_out, sem.at[0]),
        pltpu.make_async_copy(layer, layer_out, sem.at[1]),
    ]
    for c in copies:
        c.start()
    for c in copies:
        c.wait()


def fused_device(
    ctx_count, exp_count, queries, pages, cached_lengths, residual_in, out_weight, norm_gain,
    expert_ids, route_scores, expert_input, expert_output,
):
    fresh, query_width = queries.shape[1:]
    page_size = pages.shape[1]
    slab = page_size - fresh
    rows, width = residual_in.shape[1:]
    top = expert_ids.shape[2]
    hidden_width = expert_input.shape[3]
    experts = ctx_count * exp_count
    capacity = max(2, -(-rows * top // experts))
    stacked = query_width // HEAD * fresh
    vm = pl.BlockSpec(memory_space=pltpu.VMEM)
    hbm = pl.BlockSpec(memory_space=pl.ANY)
    dma = pltpu.SemaphoreType.DMA
    V = pltpu.VMEM
    lanes = exp_count * capacity
    pieces = 4
    halves = 2 if slab % 32 == 0 else 1
    blocks = stacked // HEAD
    context, layer_out = pl.pallas_call(
        functools.partial(fused_kernel, ctx_count, exp_count, capacity),
        out_shape=(V((fresh, query_width), BF), V((rows, width), BF)),
        in_specs=[hbm] * 10,
        out_specs=(vm, vm),
        scratch_shapes=[
            V((1, ctx_count), jnp.int32),
            V((2, fresh, query_width), BF),
            V((rows, width), BF),
            V((1, width), F32),
            V((top, rows), jnp.int32),
            V((top, rows), F32),
            V((ctx_count,) + pages.shape[1:], BF),
            V((ctx_count, slab, 3 * HEAD), BF),
            V((ctx_count * fresh, 3 * HEAD), BF),
            V((2, stacked, HEAD), BF),
            V((2, stacked, HEAD), F32),
            V((2, stacked, 2 * HEAD), F32),
            V((stacked, HEAD), BF),
            V((stacked, HEAD), BF),
            V((blocks, HEAD), F32),
            V((blocks, HEAD), F32),
            V(out_weight.shape, BF),
            V(expert_input.shape[1:], BF),
            V((width, hidden_width), BF),
            V((width, hidden_width), BF),
            V(expert_output.shape[1:], BF),
            V((ctx_count, top, rows), jnp.int32),
            V((ctx_count, top, rows), F32),
            V((ctx_count, top, rows), F32),
            V((ctx_count, lanes, rows), F32),
            V((ctx_count, lanes, rows), F32),
            V((pieces, fresh, width // pieces), F32),
            V((exp_count, pieces, rows, width // pieces), BF),
            V((exp_count, pieces, rows, width // pieces), BF),
            V((rows, width), BF),
            V((ctx_count, rows, width), BF),
            V((exp_count, ctx_count, capacity, width), BF),
            V((exp_count, ctx_count, capacity, width), BF),
            V((exp_count, ctx_count, capacity, width), BF),
            V((exp_count, ctx_count, capacity, width), BF),
            V((ctx_count, rows, width), BF),
            V((ctx_count, rows, width), BF),
            dma((1,)), dma((6,)), dma((3,)), dma((ctx_count, halves + 1)), dma((3,)), dma((2,)), dma((4,)),
            pltpu.SemaphoreType.REGULAR((3,)),
            dma((1,)), dma((1,)), dma((1,)), dma((1,)), dma((1,)), dma((pieces,)), dma((1,)), dma((ctx_count,)),
            dma((1,)), dma((ctx_count,)), dma((1,)), dma((ctx_count,)), dma((1,)), dma((ctx_count,)),
        ],
        compiler_params=pltpu.CompilerParams(
            collective_id=0, has_side_effects=True, vmem_limit_bytes=VMEM_LIMIT
        ),
    )(
        cached_lengths, queries[0], pages[0], residual_in[0], norm_gain.reshape(1, width),
        expert_ids[0].T, route_scores[0].T, out_weight, expert_input[0], expert_output[0],
    )
    context, layer_out = pl.pallas_call(
        settle,
        out_shape=(
            jax.ShapeDtypeStruct(context.shape, BF),
            jax.ShapeDtypeStruct(layer_out.shape, BF),
        ),
        in_specs=[vm, vm],
        out_specs=(hbm, hbm),
        scratch_shapes=[dma((2,))],
    )(
        pltpu.with_memory_space_constraint(context, pltpu.VMEM),
        pltpu.with_memory_space_constraint(layer_out, pltpu.VMEM),
    )
    return context[None], layer_out[None]


def fused_fits(mesh):
    return mesh.shape["rep"] == 1 and mesh.shape["ctx"] == 4


def solution(mesh):
    in_specs = (
        P("groups", "ctx", ("exp", "rep")),
        P("groups", "ctx", None, "exp"),
        P("groups", None),
        P("groups", ("ctx", "exp"), None),
        P(("exp", "rep"), None),
        P(),
        P("groups", ("ctx", "exp"), None),
        P("groups", ("ctx", "exp"), None),
        P(("ctx", "exp"), None, None, "rep"),
        P(("ctx", "exp"), "rep", None),
    )
    out_specs = (P("groups", "ctx", ("exp", "rep")), P("groups", ("ctx", "exp", "rep"), None))
    body = per_device
    if fused_fits(mesh):
        body = functools.partial(fused_device, mesh.shape["ctx"], mesh.shape["exp"])
    return jax.shard_map(
        body, mesh=mesh, in_specs=in_specs, out_specs=out_specs, check_vma=False
    )
```
